32 devices in a mesh: dp: 4 (over x, core), expert: 8 (over z, y).
Axes of the slice: x: 2, y: 2, z: 4, core: 2. Of those that a mesh axis runs over, the one named last changes fastest.
Arguments:
- tokens: bfloat16 [4096, 4096], P(('dp', 'expert')), may hold values from -6 to 6
- expert_ids: int32 [4096, 2], P(('dp', 'expert')), may hold values from 0 to 7, as said below
- gate_codes: int32 [4096, 2], P(('dp', 'expert')), may hold values from 1 to 64
- w_gate: bfloat16 [8, 4096, 768], P('expert'), may hold values from -0.09375 to 0.09375
- w_up: bfloat16 [8, 4096, 768], P('expert'), may hold values from -0.09375 to 0.09375
- w_down: bfloat16 [8, 768, 4096], P('expert'), may hold values from -0.21875 to 0.21875
- out_grad: bfloat16 [4096, 4096], P(('dp', 'expert')), may hold values from -6 to 6
Outputs:
- layer_out: bfloat16 [4096, 4096], P(('dp', 'expert'))
- tokens_grad: bfloat16 [4096, 4096], P(('dp', 'expert'))
- gate_weight_grad: bfloat16 [8, 4096, 768], P('expert', 'dp')
- up_weight_grad: bfloat16 [8, 4096, 768], P('expert', 'dp')
- down_weight_grad: bfloat16 [8, 768, 4096], P('expert', None, 'dp')
The draws below stay inside these ranges and needn't reach their ends.
Inputs may be any that keep to these rules, and one draw needn't show every extreme that they name: `expert_ids`: each token names 2 different experts. In the rows of one device no expert is named more than 48 times, and in every draw one and the same expert is named exactly 48 times by the rows of every device.
All inputs are finite; a program needn't handle non-finite values.
Results may differ from the reference program's by a relative error of at most 0.009.
Values may be sent and summed in bfloat16 or wider, within the bound.
A program may use at most 192 MiB of HBM per device.

```python
import jax
import jax.numpy as jnp
from jax import lax

D = 4096
HID = 768
TOPK = 2
TOK_DEV = 128
EXPERTS = 8
CAP = 48
TOKENS = 4096


def route_block(block_key, hot_expert):
    key_order, key_weight, key_tokens, key_shift = jax.random.split(block_key, 4)
    pair_count = TOK_DEV * TOPK
    spare_slots = pair_count - CAP
    shuffled = jax.random.permutation(key_order, EXPERTS).astype(jnp.int32)
    expert_range = jnp.arange(EXPERTS, dtype=jnp.int32)
    sort_score = jnp.where(shuffled == hot_expert, -1, expert_range)
    ordering = shuffled[jnp.argsort(sort_score, stable=True)]
    range_weight = jax.random.randint(key_weight, (EXPERTS,), 2, 4).astype(jnp.int32)
    range_weight = range_weight.at[0].set(0)
    running = jnp.cumsum(range_weight)
    bounds = CAP + spare_slots * running // running[-1]
    slot_index = jnp.arange(pair_count, dtype=jnp.int32)
    slot_shift = jax.random.randint(key_shift, (), 0, pair_count).astype(jnp.int32)
    rotated = (slot_index + slot_shift) % pair_count
    position = jnp.sum((rotated[:, None] >= bounds[None, :]).astype(jnp.int32), axis=1)
    chosen = ordering[position]
    pair_table = chosen.reshape(TOPK, TOK_DEV).T
    token_order = jax.random.permutation(key_tokens, TOK_DEV).astype(jnp.int32)
    inverse = jnp.argsort(token_order, stable=True)
    return pair_table[inverse]


def draw_expert_ids(key, part):
    key_hot, key_blocks = jax.random.split(jax.random.fold_in(key, 17))
    hot_expert = jax.random.randint(key_hot, (), 0, EXPERTS).astype(jnp.int32)
    block_keys = jax.random.split(key_blocks, TOKENS // TOK_DEV)
    tables = jax.vmap(route_block, in_axes=(0, None))(block_keys, hot_expert)
    return tables.reshape(TOKENS, TOPK).astype(jnp.int32)


def touch_ends(values, rng, smallest, high):
    longest = values.shape.index(max(values.shape))
    spots = []
    for shift in (0, 1):
        where = [jax.random.randint(jax.random.fold_in(rng, axis), (), 0, length) for axis, length in enumerate(values.shape)]
        where[longest] = (where[longest] + shift) % values.shape[longest]
        spots.append(tuple(where))
    return values.at[spots[0]].set(smallest).at[spots[1]].set(high)


def levels(own_key, shape, shards, low, top_value):
    gain, own = 1.0, jax.random.fold_in(own_key, 6)
    for dim, parts in shards:
        draws = jnp.exp(jax.random.uniform(jax.random.fold_in(own, dim), (parts,), jnp.float32, low / len(shards), top_value / len(shards)))
        gain = gain * jnp.repeat(draws, shape[dim] // parts).reshape([-1 if axis == dim else 1 for axis in range(len(shape))])
    return gain


def centred(key, shape, scale, most, pieces=(), held_as=jnp.bfloat16):
    drawn = scale * jax.random.normal(key, shape, jnp.float32)
    if pieces:
        drawn = drawn * levels(key, shape, pieces, -0.22, 0.18)
    return jnp.clip(drawn, -most, most).astype(held_as)


def setup_inputs(seed: int = 0) -> dict:
    key_of = jax.random.split(jax.random.key(seed), 8)
    tokens = centred(key_of[0], (TOKENS, D), 1.0, 6.0, ((0, 32),))
    expert_ids = draw_expert_ids(jax.random.fold_in(key_of[7], 71), 0)
    gate_codes = touch_ends(jax.random.randint(key_of[2], (TOKENS, TOPK), 1, 65), jax.random.fold_in(key_of[2], 1), 1, 64).astype(jnp.int32)
    w_gate = centred(key_of[3], (EXPERTS, D, HID), D ** -0.5, 0.09375, ((0, 8),))
    w_up = centred(key_of[4], (EXPERTS, D, HID), D ** -0.5, 0.09375, ((0, 8),))
    w_down = centred(key_of[5], (EXPERTS, HID, D), HID ** -0.5, 0.21875, ((0, 8),))
    out_grad = centred(key_of[6], (TOKENS, D), 1.0, 6.0, ((0, 32),))
    return dict(tokens=tokens, expert_ids=expert_ids, gate_codes=gate_codes, w_gate=w_gate, w_up=w_up, w_down=w_down, out_grad=out_grad)


def slot_targets(block_ids):
    flat_ids = block_ids.reshape(-1)
    one_hot = (flat_ids[:, None] == jnp.arange(EXPERTS, dtype=jnp.int32)[None, :]).astype(jnp.int32)
    earlier = jnp.cumsum(one_hot, axis=0) - one_hot
    slot_ranks = jnp.sum(earlier * one_hot, axis=1)
    return (flat_ids * CAP + slot_ranks).astype(jnp.int32)


def owner_table(targets):
    pair_count = targets.shape[0]
    return jnp.full((EXPERTS * CAP,), -1, jnp.int32).at[targets].set(jnp.arange(pair_count, dtype=jnp.int32))


def group_sums(left_rows, right_rows, group_count):
    left_rows = left_rows.reshape(group_count, EXPERTS * CAP, left_rows.shape[-1]).astype(jnp.float32)
    right_rows = right_rows.reshape(group_count, EXPERTS * CAP, right_rows.shape[-1]).astype(jnp.float32)
    partials = jnp.einsum("gri,grj->gij", left_rows, right_rows)
    partials = lax.optimization_barrier(partials.astype(jnp.bfloat16)).astype(jnp.float32)
    return jnp.sum(partials, axis=0).astype(jnp.bfloat16)


def reference(tokens, expert_ids, gate_codes, w_gate, w_up, w_down, out_grad):
    block_count = TOKENS // TOK_DEV
    group_count = block_count // EXPERTS
    pair_count = TOK_DEV * TOPK
    token_blocks = tokens.reshape(block_count, TOK_DEV, D)
    grad_blocks = out_grad.reshape(block_count, TOK_DEV, D)
    gate_blocks = gate_codes.astype(jnp.float32).reshape(block_count, pair_count) / 64.0
    targets = jax.vmap(slot_targets)(expert_ids.reshape(block_count, TOK_DEV, TOPK))
    owners = jax.vmap(owner_table)(targets).reshape(block_count, EXPERTS, CAP)
    block_index = jnp.arange(block_count, dtype=jnp.int32)[:, None]
    contract = (((1,), (1,)), ((), ()))

    def one_expert(carry, expert):
        out_total, grad_total = carry
        slot_pairs = lax.dynamic_index_in_dim(owners, expert, 1, keepdims=False)
        is_live = slot_pairs >= 0
        safe_pair = jnp.maximum(slot_pairs, 0)
        token_pos = safe_pair // TOPK
        pair_gains = jnp.where(is_live, jnp.take_along_axis(gate_blocks, safe_pair, axis=1), 0.0)
        gate_matrix = lax.dynamic_index_in_dim(w_gate, expert, 0, keepdims=False)
        up_matrix = lax.dynamic_index_in_dim(w_up, expert, 0, keepdims=False)
        down_matrix = lax.dynamic_index_in_dim(w_down, expert, 0, keepdims=False)
        picked = token_blocks[block_index, token_pos]
        picked = jnp.where(is_live[..., None], picked, jnp.zeros((), jnp.bfloat16)).reshape(block_count * CAP, D)
        pre_gate = jnp.dot(picked, gate_matrix, preferred_element_type=jnp.float32)
        pre_up = jnp.dot(picked, up_matrix, preferred_element_type=jnp.float32)
        sigmoid_gate = jax.nn.sigmoid(pre_gate)
        silu_gate = pre_gate * sigmoid_gate
        hidden = (silu_gate * pre_up).astype(jnp.bfloat16)
        expert_out = jnp.dot(hidden, down_matrix, preferred_element_type=jnp.float32).astype(jnp.bfloat16)
        expert_out = expert_out.reshape(block_count, CAP, D)
        upstream = grad_blocks[block_index, token_pos]
        pair_grad = (pair_gains[..., None] * upstream.astype(jnp.float32)).astype(jnp.bfloat16)
        pair_grad = pair_grad.reshape(block_count * CAP, D)
        hidden_grad = lax.dot_general(pair_grad, down_matrix, contract, preferred_element_type=jnp.float32)
        gate_pre_grad = (hidden_grad * pre_up * sigmoid_gate * (1.0 + pre_gate * (1.0 - sigmoid_gate))).astype(jnp.bfloat16)
        up_pre_grad = (hidden_grad * silu_gate).astype(jnp.bfloat16)
        input_grad = lax.dot_general(gate_pre_grad, gate_matrix, contract, preferred_element_type=jnp.float32)
        input_grad = input_grad + lax.dot_general(up_pre_grad, up_matrix, contract, preferred_element_type=jnp.float32)
        input_grad = input_grad.astype(jnp.bfloat16).reshape(block_count, CAP, D)
        weighted = pair_gains[..., None] * expert_out.astype(jnp.float32)
        out_total = out_total.at[block_index, token_pos].add(weighted)
        masked_grad = jnp.where(is_live[..., None], input_grad.astype(jnp.float32), 0.0)
        grad_total = grad_total.at[block_index, token_pos].add(masked_grad)
        gate_sum = group_sums(picked, gate_pre_grad, group_count)
        up_sum = group_sums(picked, up_pre_grad, group_count)
        down_sum = group_sums(hidden, pair_grad, group_count)
        return (out_total, grad_total), (gate_sum, up_sum, down_sum)

    start_total = jnp.zeros((block_count, TOK_DEV, D), jnp.float32)
    carried, stacked = lax.scan(one_expert, (start_total, start_total), jnp.arange(EXPERTS, dtype=jnp.int32))
    layer_out = carried[0].astype(jnp.bfloat16).reshape(TOKENS, D)
    tokens_grad = carried[1].astype(jnp.bfloat16).reshape(TOKENS, D)
    return (layer_out, tokens_grad, stacked[0], stacked[1], stacked[2])
```

```python
import functools

import jax
import jax.numpy as jnp
from jax import lax
from jax.experimental import pallas as pl
from jax.experimental.pallas import tpu as pltpu
from jax.sharding import PartitionSpec as P

F32 = jnp.float32
BF16 = jnp.bfloat16
CONTRACT = (((1,), (1,)), ((), ()))
ROWS_FIRST = (((0,), (0,)), ((), ()))
LINE = 4
MIB = 2**20


def remote(src, dst, send, recv, peer):
    return pltpu.make_async_remote_copy(src_ref=src, dst_ref=dst, send_sem=send, recv_sem=recv, device_id=peer)


def exchange_kernel(
    lanes, cap, groups, chunks, ring,
    ids, codes, tokens, out_grad, w_gate, w_up, w_down,
    layer_out, tokens_grad, token_cols, grad_cols, all_hidden, all_gate, all_up,
    info, raw, sel, selt, half_selt, plane, mate_stage, landed, pre_gate, pre_up, hidden_grad,
    hidden, gate_pre, up_pre, vdown, vgate, vup, made, back, part_out, part_in, fin_out, out_stage,
    info_send, info_recv, raw_load, raw_send, raw_recv, forward_send, plane_send, plane_recv,
    mate_send, mate_recv, made_send, made_recv, back_send, back_recv, part_send, part_recv,
    fin_send, fin_recv, out_sem, weight_sem, down_sem, group_send, group_recv, act_send, act_recv,
):
    me = lax.axis_index("expert")
    group = lax.axis_index("dp")
    z = me // lanes
    y = me - z * lanes
    inner = (z + 1) // 2 == 1
    outer = (z + 1) // 2 != 1
    mate_z = z + 1 - 2 * lax.rem(z, 2)
    far_z = LINE - 1 - z
    mate = {"expert": mate_z * lanes + y}
    far = {"expert": far_z * lanes + y}
    onward = {"expert": jnp.where(inner, far_z, mate_z) * lanes + y}
    onward_slot = jnp.where(inner, 2, 1)
    experts = LINE * lanes
    tok_count, model_width = tokens.shape
    width = model_width // chunks
    block = model_width // groups
    per_block = chunks // groups
    pieces = 2 * chunks
    half = lanes * cap
    quad = LINE * cap
    sources = (tokens, out_grad)

    def lane_peer(j):
        return lax.rem(y + j, lanes)

    def group_peer(shift):
        return {"dp": lax.rem(group + shift, groups)}

    def place(n):
        order, inside = divmod(n % chunks, per_block)
        return (order + 1) % groups, inside

    def columns(n):
        shift, inside = place(n)
        start = lax.rem(group + shift, groups) * block + inside * width
        return pl.ds(pl.multiple_of(start, 128), width)

    def lane_rows(index, count):
        return pl.ds(pl.multiple_of(index * count, 16), count)

    def weight_loads(u):
        at, slot = columns(u), u % ring
        return (
            pltpu.make_async_copy(w_gate.at[at, :], vgate.at[slot], weight_sem.at[u, 0]),
            pltpu.make_async_copy(w_up.at[at, :], vup.at[slot], weight_sem.at[u, 1]),
        )

    def down_load(q):
        return pltpu.make_async_copy(w_down.at[:, columns(q)], vdown.at[q], down_sem.at[q])

    loads, onwards, forwards, mates, planes = [], [], [], [], []
    from_mate_raw, from_far_raw = [], []
    for n in range(pieces):
        c = n % chunks
        source = sources[n // chunks].at[:, columns(n)]
        loads.append(pltpu.make_async_copy(source, raw.at[0, c], raw_load.at[n]))
        onwards.append(remote(source, raw.at[onward_slot, c], raw_send.at[n], raw_recv.at[n, onward_slot], onward))
        forwards.append(remote(raw.at[1, c], raw.at[3, c], forward_send.at[n], raw_recv.at[n, 3], far))
        from_mate_raw.append(remote(raw.at[1, c], raw.at[1, c], raw_send.at[n], raw_recv.at[n, 1], mate))
        from_far_raw.append(remote(raw.at[2, c], raw.at[2, c], raw_send.at[n], raw_recv.at[n, 2], far))
        mates.append(
            remote(mate_stage.at[c], plane.at[c, :, pl.ds(cap, 3 * cap)], mate_send.at[n], mate_recv.at[n], mate)
        )
        planes.append([
            remote(
                plane.at[c, lane_peer(j)], landed.at[n, lane_rows(y, quad)],
                plane_send.at[n, j - 1], plane_recv.at[n, j - 1], {"expert": z * lanes + lane_peer(j)},
            )
            for j in range(1, lanes)
        ])
    mades, backs, parts, fins, outs = [], [], [], [], []
    for m in range(pieces):
        c = m % chunks
        mades.append([
            remote(
                made.at[c, lane_peer(j)], back.at[c, :, lane_rows(y, cap)],
                made_send.at[m, j - 1], made_recv.at[m, j - 1], {"expert": z * lanes + lane_peer(j)},
            )
            for j in range(1, lanes)
        ])
        own_part, mate_part = pl.ds(0, half), pl.ds(half, half)
        backs.append([
            remote(back.at[c, 1, own_part], back.at[c, 0, mate_part], back_send.at[m, 0], back_recv.at[m, 0], mate),
            remote(
                back.at[c, pl.ds(2, 2), own_part], back.at[c, pl.ds(2, 2), mate_part],
                back_send.at[m, 1], back_recv.at[m, 1], mate,
            ),
        ])
        parts.append(remote(part_out.at[c], part_in.at[c], part_send.at[m], part_recv.at[m], far))
        fins.append(remote(fin_out.at[c], part_in.at[c, 0], fin_send.at[m], fin_recv.at[m], mate))
        target = (layer_out, tokens_grad)[m // chunks]
        outs.append(pltpu.make_async_copy(out_stage.at[m % 4], target.at[:, columns(m)], out_sem.at[m]))
    info_onward = remote(info.at[0], info.at[onward_slot], info_send.at[0], info_recv.at[onward_slot], onward)
    info_forward = remote(info.at[1], info.at[3], info_send.at[1], info_recv.at[3], far)
    info_from_mate = remote(info.at[1], info.at[1], info_send.at[0], info_recv.at[1], mate)
    info_from_far = remote(info.at[2], info.at[2], info_send.at[0], info_recv.at[2], far)

    group_copies = []

    def to_group(source, target, shift, send, recv):
        if shift == 0:
            copy = pltpu.make_async_copy(source, target, send)
        else:
            copy = remote(source, target, send, recv, group_peer(shift))
        copy.start()
        group_copies.append((shift, copy))

    for n in range(2):
        loads[n].start()
    for u in range(ring):
        for load in weight_loads(u):
            load.start()
    barrier = pltpu.get_barrier_semaphore()
    for shift in range(1, groups):
        pl.semaphore_signal(barrier, inc=1, device_id=group_peer(shift))
    for j in range(1, lanes):
        pl.semaphore_signal(barrier, inc=1, device_id={"expert": z * lanes + lane_peer(j)})
    pl.semaphore_signal(barrier, inc=1, device_id=mate)

    @pl.when(inner)
    def _():
        pl.semaphore_signal(barrier, inc=1, device_id=far)
        pl.semaphore_wait(barrier, lanes + groups)

    @pl.when(outer)
    def _():
        pl.semaphore_wait(barrier, lanes + groups - 1)

    onwards[0].start()
    onwards[1].start()

    expert_range = lax.broadcasted_iota(jnp.int32, (experts, tok_count), 0)
    named = [ids[k : k + 1, :] == expert_range for k in range(2)]
    chosen = jnp.where(named[0], 1.0, 0.0) + jnp.where(named[1], 1.0, 0.0)
    before = lax.broadcasted_iota(jnp.int32, (tok_count, tok_count), 0)
    after = lax.broadcasted_iota(jnp.int32, (tok_count, tok_count), 1)
    earlier = jnp.where(before < after, 1.0, 0.0).astype(BF16)
    ranks = jnp.dot(chosen.astype(BF16), earlier, preferred_element_type=F32)
    info[0, 0:experts] = jnp.where(chosen > 0.5, ranks, -1.0)
    gates = [jnp.where(named[k], codes[k : k + 1, :].astype(F32), 0.0) for k in range(2)]
    info[0, experts : 2 * experts] = (gates[0] + gates[1]) * (1.0 / 64.0)
    info_onward.start()
    for q in range(chunks):
        down_load(q).start()

    slot_range = lax.broadcasted_iota(jnp.int32, (cap, tok_count), 0).astype(F32)
    diagonal = jnp.where(before == after, 1.0, 0.0).astype(BF16)

    def select(s, planes_used):
        for p in range(planes_used):
            for lane in range(lanes):
                expert = (z, mate_z)[p] * lanes + lane
                hit = info[s, pl.ds(expert, 1), :] == slot_range
                gate = info[s, pl.ds(experts + expert, 1), :]
                at = pl.ds(p * half + lane * cap, cap)
                sel[0, s, at] = jnp.where(hit, 1.0, 0.0).astype(BF16)
                sel[1, s, at] = jnp.where(hit, gate, 0.0).astype(BF16)
        for kind in range(2):
            matrix = sel[kind, s, 0 : planes_used * half]
            turned = lax.dot_general(diagonal, matrix, CONTRACT, preferred_element_type=F32).astype(BF16)
            if planes_used == 2:
                selt[kind, s] = turned
            else:
                half_selt[kind] = turned

    @pl.when(inner)
    def _():
        select(0, 2)
        info_from_mate.wait_recv()
        info_forward.start()
        select(1, 1)
        info_from_far.wait_recv()
        select(2, 2)
        info_forward.wait_recv()
        select(3, 2)
        info_forward.wait_send()

    @pl.when(outer)
    def _():
        select(0, 1)

    info_onward.wait_send()

    def spread(n, s, start, count):
        kind = n // chunks
        values = jnp.dot(
            sel[kind, s, start : start + count], raw[s, n % chunks], preferred_element_type=F32
        )
        return values.astype(BF16)

    def into_plane(n, s, values):
        for lane in range(lanes):
            plane[n % chunks, lane, s * cap : (s + 1) * cap] = values[lane * cap : (lane + 1) * cap]

    def keep_own(n):
        for copy in planes[n]:
            copy.start()
        landed[n, lane_rows(y, quad)] = plane[n % chunks, y]

    def stage_forward(n):
        @pl.when(inner)
        def _():
            from_mate_raw[n].wait_recv()
            forwards[n].start()

    def stage_spread(n):
        c = n % chunks
        loads[n].wait()

        @pl.when(inner)
        def _():
            if n >= 1:
                forwards[n - 1].wait_send()
            if n >= chunks:
                mates[n - chunks].wait_send()
            both = spread(n, 0, 0, 2 * half)
            into_plane(n, 0, both[:half])
            mine = [both[half:]]
            into_plane(n, 1, spread(n, 1, 0, half))
            from_far_raw[n].wait_recv()
            both = spread(n, 2, 0, 2 * half)
            into_plane(n, 2, both[:half])
            mine.append(both[half:])
            forwards[n].wait_recv()
            both = spread(n, 3, 0, 2 * half)
            into_plane(n, 3, both[:half])
            mine.append(both[half:])
            for k in range(3):
                for lane in range(lanes):
                    mate_stage[c, lane, k * cap : (k + 1) * cap] = mine[k][lane * cap : (lane + 1) * cap]
            mates[n].start()
            keep_own(n)

        @pl.when(outer)
        def _():
            into_plane(n, 0, spread(n, 0, 0, half))

    def stage_relay(n):
        @pl.when(outer)
        def _():
            mates[n].wait_recv()
            keep_own(n)

    def stage_multiply(n):
        q = n % chunks
        for copy in planes[n]:
            copy.wait_recv()
        shift, inside = place(n)
        target = (token_cols, grad_cols)[n // chunks]
        to_group(
            landed.at[n], target.at[shift, :, pl.ds(inside * width, width)], shift, group_send.at[n], group_recv.at[n]
        )
        rows = landed[n]
        if n < chunks:
            for load in weight_loads(n):
                load.wait()
            for total, matrix in ((pre_gate, vgate), (pre_up, vup)):
                term = jnp.dot(rows, matrix[n % ring], preferred_element_type=F32)
                total[...] = term if q == 0 else total[...] + term
            for load in weight_loads(n + ring):
                load.start()
            if q == chunks - 1:
                for start in range(0, pre_gate.shape[0], cap):
                    at = pl.ds(start, cap)
                    gate = pre_gate[at, :]
                    hidden[at, :] = (gate * jax.nn.sigmoid(gate) * pre_up[at, :]).astype(BF16)
                send_act(0, hidden, all_hidden)
        else:
            if n == chunks:
                for p in range(chunks):
                    down_load(p).wait()
            term = lax.dot_general(rows, vdown[q], CONTRACT, preferred_element_type=F32)
            hidden_grad[...] = term if q == 0 else hidden_grad[...] + term
            if q == chunks - 1:
                for start in range(0, pre_gate.shape[0], cap):
                    at = pl.ds(start, cap)
                    gate, up, grad = pre_gate[at, :], pre_up[at, :], hidden_grad[at, :]
                    sigmoid = jax.nn.sigmoid(gate)
                    silu = gate * sigmoid
                    gate_pre[at, :] = (grad * up * sigmoid * (1.0 + gate * (1.0 - sigmoid))).astype(BF16)
                    up_pre[at, :] = (grad * silu).astype(BF16)
                send_act(1, gate_pre, all_gate)
                send_act(2, up_pre, all_up)

    def send_act(kind, source, target):
        for order in range(groups):
            shift = (order + 1) % groups
            to_group(source, target.at[shift], shift, act_send.at[kind, shift], act_recv.at[kind, shift])

    def stage_make(m):
        c = m % chunks
        if m < chunks:
            values = jnp.dot(hidden[...], vdown[c], preferred_element_type=F32)
        else:
            slot = m % ring
            for load in weight_loads(m):
                load.wait()
            values = lax.dot_general(gate_pre[...], vgate[slot], CONTRACT, preferred_element_type=F32)
            values = values + lax.dot_general(up_pre[...], vup[slot], CONTRACT, preferred_element_type=F32)
            if m + ring < pieces:
                for load in weight_loads(m + ring):
                    load.start()
            for copy in mades[m - chunks]:
                copy.wait_send()
        made[c] = values.astype(BF16).reshape(lanes, LINE, cap, width)
        for copy in mades[m]:
            copy.start()
        back[c, :, lane_rows(y, cap)] = made[c, y]

    def stage_hand(m):
        @pl.when(outer)
        def _():
            for copy in mades[m]:
                copy.wait_recv()
            for copy in backs[m]:
                copy.start()

    def gather(m, s):
        kind = 1 - m // chunks
        return jnp.dot(selt[kind, s], back[m % chunks, s], preferred_element_type=F32)

    def gather_half(m, s):
        kind = 1 - m // chunks
        return jnp.dot(half_selt[kind], back[m % chunks, s, 0:half], preferred_element_type=F32)

    def stage_partial(m):
        c = m % chunks

        @pl.when(inner)
        def _():
            for copy in mades[m]:
                copy.wait_recv()
            for copy in backs[m]:
                copy.wait_recv()
            if m >= chunks:
                parts[m - chunks].wait_send()
            for s in (2, 3):
                part_out[c, s - 2] = gather(m, s).astype(BF16)
            parts[m].start()

    def stage_finish(m):
        c = m % chunks
        if m >= 4:
            outs[m - 4].wait()

        @pl.when(inner)
        def _():
            if m >= chunks:
                fins[m - chunks].wait_send()
            near = gather_half(m, 1)
            own = gather(m, 0)
            parts[m].wait_recv()
            fin_out[c] = (near + part_in[c, 1].astype(F32)).astype(BF16)
            fins[m].start()
            out_stage[m % 4] = (own + part_in[c, 0].astype(F32)).astype(BF16)

        @pl.when(outer)
        def _():
            near = gather_half(m, 0)
            for copy in backs[m]:
                copy.wait_send()
            fins[m].wait_recv()
            out_stage[m % 4] = (near + part_in[c, 0].astype(F32)).astype(BF16)

        outs[m].start()

    stage_forward(0)
    first_make = chunks + 2
    for tick in range(first_make + pieces + 3):
        n = tick + 2
        if n < pieces:
            if n >= chunks:
                for copy in planes[n - chunks]:
                    copy.wait_send()
            loads[n].start()
            onwards[n].start()
        m = tick - first_make
        if 0 <= m - 1 < pieces:
            stage_hand(m - 1)
        if 0 <= m - 2 < pieces:
            stage_partial(m - 2)
        if tick + 1 < pieces:
            stage_forward(tick + 1)
        if tick < pieces:
            stage_spread(tick)
        if 0 <= tick - 1 < pieces:
            stage_relay(tick - 1)
        if 0 <= tick - 2 < pieces:
            stage_multiply(tick - 2)
        if 0 <= m < pieces:
            stage_make(m)
        if 0 <= m - 3 < pieces:
            stage_finish(m - 3)

    for n in range(pieces):
        onwards[n].wait_send()
    for n in range(chunks, pieces):
        for copy in planes[n]:
            copy.wait_send()
    for m in range(chunks, pieces):
        for copy in mades[m]:
            copy.wait_send()
    for m in range(pieces - 4, pieces):
        outs[m].wait()

    @pl.when(inner)
    def _():
        forwards[pieces - 1].wait_send()
        for n in range(chunks, pieces):
            mates[n].wait_send()
        for m in range(chunks, pieces):
            parts[m].wait_send()
            fins[m].wait_send()

    for shift, copy in group_copies:
        if shift == 0:
            copy.wait()
        else:
            copy.wait_recv()
            copy.wait_send()


def weights_kernel(
    layer_in, tokens_in, token_cols, grad_cols, all_hidden, all_gate, all_up,
    layer_out, tokens_grad, gate_sum, up_sum, down_sum,
    left, grads, acts, result, load_sem, move_sem, out_sem,
):
    moves = [
        pltpu.make_async_copy(a, b, move_sem.at[i])
        for i, (a, b) in enumerate(((layer_in, layer_out), (tokens_in, tokens_grad)))
    ]
    pairs = (
        (all_hidden, acts.at[0]), (grad_cols, grads), (token_cols, left), (all_gate, acts.at[1]), (all_up, acts.at[2])
    )
    loads = [pltpu.make_async_copy(a, b, load_sem.at[i]) for i, (a, b) in enumerate(pairs)]
    for copy in loads + moves:
        copy.start()
    depth = left.shape[0] * left.shape[1]
    block = left.shape[2]
    units = acts.shape[3]
    tile = 256
    stores = []

    def matrix(ref, at):
        return ref[:, :, at].reshape(depth, at.size)

    def put(values, target):
        i = len(stores)
        slot = i % 2
        if i >= 2:
            stores[i - 2].wait()
        result[slot, :, 0 : values.shape[1]] = values.astype(BF16)
        copy = pltpu.make_async_copy(result.at[slot, :, pl.ds(0, values.shape[1])], target, out_sem.at[i])
        copy.start()
        stores.append(copy)

    loads[0].wait()
    loads[1].wait()
    for start in range(0, units, tile):
        at = pl.ds(start, tile)
        values = lax.dot_general(
            matrix(acts.at[0], at), matrix(grads, pl.ds(0, block)), ROWS_FIRST, preferred_element_type=F32
        )
        put(values, down_sum.at[at, :])
    loads[2].wait()
    for kind, target in ((1, gate_sum), (2, up_sum)):
        loads[2 + kind].wait()
        for start in range(0, block, tile):
            at = pl.ds(start, tile)
            values = lax.dot_general(
                matrix(left, at), matrix(acts.at[kind], pl.ds(0, units)), ROWS_FIRST, preferred_element_type=F32
            )
            put(values, target.at[at, :])
    for copy in stores[-2:] + moves:
        copy.wait()


def per_device(tokens, expert_ids, gate_codes, w_gate, w_up, w_down, out_grad):
    experts = lax.axis_size("expert")
    groups = lax.axis_size("dp")
    lanes = experts // LINE
    tok_count, model_width = tokens.shape
    pair_count = tok_count * expert_ids.shape[1]
    capacity = 3 * pair_count // (2 * experts)
    capacity = -(-capacity // 16) * 16
    rows = experts * capacity
    half = lanes * capacity
    chunks = groups * max(1, 8 // groups)
    ring = chunks // 2
    width = model_width // chunks
    block = model_width // groups
    pieces = 2 * chunks
    gate_matrix, up_matrix, down_matrix = w_gate[0], w_up[0], w_down[0]
    units = gate_matrix.shape[1]
    vmem = pl.BlockSpec(memory_space=pltpu.VMEM)
    anywhere = pl.BlockSpec(memory_space=pl.ANY)
    dma = pltpu.SemaphoreType.DMA

    def shape(*dims):
        return jax.ShapeDtypeStruct(dims, BF16)

    def buffer(*dims):
        return pltpu.VMEM(dims, BF16)

    peers = max(1, lanes - 1)
    layer_out, tokens_grad, *factors = pl.pallas_call(
        functools.partial(exchange_kernel, lanes, capacity, groups, chunks, ring),
        out_shape=(
            shape(tok_count, model_width),
            shape(tok_count, model_width),
            shape(groups, rows, block),
            shape(groups, rows, block),
            shape(groups, rows, units),
            shape(groups, rows, units),
            shape(groups, rows, units),
        ),
        in_specs=[vmem] * 2 + [anywhere] * 5,
        out_specs=(anywhere,) * 7,
        scratch_shapes=[
            pltpu.VMEM((LINE, 2 * experts, tok_count), F32),
            buffer(LINE, chunks, tok_count, width),
            buffer(2, LINE, 2 * half, tok_count),
            buffer(2, LINE, tok_count, 2 * half),
            buffer(2, tok_count, half),
            buffer(chunks, lanes, LINE * capacity, width),
            buffer(chunks, lanes, 3 * capacity, width),
            buffer(pieces, rows, width),
            pltpu.VMEM((rows, units), F32),
            pltpu.VMEM((rows, units), F32),
            pltpu.VMEM((rows, units), F32),
            buffer(rows, units),
            buffer(rows, units),
            buffer(rows, units),
            buffer(chunks, units, width),
            buffer(ring, width, units),
            buffer(ring, width, units),
            buffer(chunks, lanes, LINE, capacity, width),
            buffer(chunks, LINE, 2 * half, width),
            buffer(chunks, 2, tok_count, width),
            buffer(chunks, 2, tok_count, width),
            buffer(chunks, tok_count, width),
            buffer(4, tok_count, width),
            dma((2,)),
            dma((LINE,)),
            dma((pieces,)),
            dma((pieces,)),
            dma((pieces, LINE)),
            dma((pieces,)),
            dma((pieces, peers)),
            dma((pieces, peers)),
            dma((pieces,)),
            dma((pieces,)),
            dma((pieces, peers)),
            dma((pieces, peers)),
            dma((pieces, 2)),
            dma((pieces, 2)),
            dma((pieces,)),
            dma((pieces,)),
            dma((pieces,)),
            dma((pieces,)),
            dma((pieces,)),
            dma((pieces, 2)),
            dma((chunks,)),
            dma((pieces,)),
            dma((pieces,)),
            dma((3, groups)),
            dma((3, groups)),
        ],
        compiler_params=pltpu.CompilerParams(
            collective_id=0, has_side_effects=True, vmem_limit_bytes=63 * MIB
        ),
    )(expert_ids.T, gate_codes.T, tokens, out_grad, gate_matrix, up_matrix, down_matrix)

    outs = pl.pallas_call(
        weights_kernel,
        out_shape=(
            shape(tok_count, model_width),
            shape(tok_count, model_width),
            shape(block, units),
            shape(block, units),
            shape(units, block),
        ),
        in_specs=[anywhere] * 7,
        out_specs=(anywhere,) * 5,
        scratch_shapes=[
            buffer(groups, rows, block),
            buffer(groups, rows, block),
            buffer(3, groups, rows, units),
            buffer(2, 256, max(block, units)),
            dma((5,)),
            dma((2,)),
            dma((units // 256 + 2 * (block // 256),)),
        ],
        compiler_params=pltpu.CompilerParams(vmem_limit_bytes=56 * MIB),
    )(layer_out, tokens_grad, *factors)
    layer_out, tokens_grad, gate_sum, up_sum, down_sum = outs
    return layer_out, tokens_grad, gate_sum[None], up_sum[None], down_sum[None]


def solution(mesh):
    placed = (
        P(("dp", "expert"), None),
        P(("dp", "expert"), None),
        P(("dp", "expert"), None),
        P("expert", None, None),
        P("expert", None, None),
        P("expert", None, None),
        P(("dp", "expert"), None),
    )
    return jax.shard_map(
        per_device,
        mesh=mesh,
        in_specs=placed,
        out_specs=(
            P(("dp", "expert"), None),
            P(("dp", "expert"), None),
            P("expert", "dp", None),
            P("expert", "dp", None),
            P("expert", None, "dp"),
        ),
        check_vma=False,
    )
```

```python
import functools

import jax
import jax.numpy as jnp
from jax import lax
from jax.experimental import pallas as pl
from jax.experimental.pallas import tpu as pltpu
from jax.sharding import PartitionSpec as P

F32 = jnp.float32
BF16 = jnp.bfloat16
CONTRACT = (((1,), (1,)), ((), ()))
ROWS_FIRST = (((0,), (0,)), ((), ()))
LINE = 4
MIB = 2**20


def remote(src, dst, send, recv, peer):
    return pltpu.make_async_remote_copy(src_ref=src, dst_ref=dst, send_sem=send, recv_sem=recv, device_id=peer)


def exchange_kernel(
    lanes, cap, groups, chunks, ring,
    ids, codes, tokens, out_grad, w_gate, w_up, w_down,
    layer_out, tokens_grad, token_cols, grad_cols, all_hidden, all_gate, all_up,
    info, raw, sel, selt, half_selt, plane, mate_stage, landed, pre_gate, pre_up, hidden_grad,
    hidden, gate_pre, up_pre, vdown, vgate, vup, made, back, part_out, part_in, fin_out, out_stage,
    info_send, info_recv, raw_load, raw_send, raw_recv, forward_send, plane_send, plane_recv,
    mate_send, mate_recv, made_send, made_recv, back_send, back_recv, part_send, part_recv,
    fin_send, fin_recv, out_sem, weight_sem, down_sem, group_send, group_recv, act_send, act_recv,
):
    me = lax.axis_index("expert")
    group = lax.axis_index("dp")
    z = me // lanes
    y = me - z * lanes
    inner = (z + 1) // 2 == 1
    outer = (z + 1) // 2 != 1
    mate_z = z + 1 - 2 * lax.rem(z, 2)
    far_z = LINE - 1 - z
    mate = {"expert": mate_z * lanes + y}
    far = {"expert": far_z * lanes + y}
    onward = {"expert": jnp.where(inner, far_z, mate_z) * lanes + y}
    onward_slot = jnp.where(inner, 2, 1)
    experts = LINE * lanes
    tok_count, model_width = tokens.shape
    width = model_width // chunks
    block = model_width // groups
    per_block = chunks // groups
    pieces = 2 * chunks
    half = lanes * cap
    quad = LINE * cap
    sources = (tokens, out_grad)

    def lane_peer(j):
        return lax.rem(y + j, lanes)

    def group_peer(shift):
        return {"dp": lax.rem(group + shift, groups)}

    def place(n):
        order, inside = divmod(n % chunks, per_block)
        return (order + 1) % groups, inside

    def columns(n):
        shift, inside = place(n)
        start = lax.rem(group + shift, groups) * block + inside * width
        return pl.ds(pl.multiple_of(start, 128), width)

    def lane_rows(index, count):
        return pl.ds(pl.multiple_of(index * count, 16), count)

    def weight_loads(u):
        at, slot = columns(u), u % ring
        return (
            pltpu.make_async_copy(w_gate.at[at, :], vgate.at[slot], weight_sem.at[u, 0]),
            pltpu.make_async_copy(w_up.at[at, :], vup.at[slot], weight_sem.at[u, 1]),
        )

    def down_load(q):
        return pltpu.make_async_copy(w_down.at[:, columns(q)], vdown.at[q], down_sem.at[q])

    loads, onwards, forwards, mates, planes = [], [], [], [], []
    from_mate_raw, from_far_raw = [], []
    for n in range(pieces):
        c = n % chunks
        source = sources[n // chunks].at[:, columns(n)]
        loads.append(pltpu.make_async_copy(source, raw.at[0, c], raw_load.at[n]))
        onwards.append(remote(source, raw.at[onward_slot, c], raw_send.at[n], raw_recv.at[n, onward_slot], onward))
        forwards.append(remote(raw.at[1, c], raw.at[3, c], forward_send.at[n], raw_recv.at[n, 3], far))
        from_mate_raw.append(remote(raw.at[1, c], raw.at[1, c], raw_send.at[n], raw_recv.at[n, 1], mate))
        from_far_raw.append(remote(raw.at[2, c], raw.at[2, c], raw_send.at[n], raw_recv.at[n, 2], far))
        mates.append(
            remote(mate_stage.at[c], plane.at[c, :, pl.ds(cap, 3 * cap)], mate_send.at[n], mate_recv.at[n], mate)
        )
        planes.append([
            remote(
                plane.at[c, lane_peer(j)], landed.at[n, lane_rows(y, quad)],
                plane_send.at[n, j - 1], plane_recv.at[n, j - 1], {"expert": z * lanes + lane_peer(j)},
            )
            for j in range(1, lanes)
        ])
    mades, backs, parts, fins, outs = [], [], [], [], []
    for m in range(pieces):
        c = m % chunks
        mades.append([
            remote(
                made.at[c, lane_peer(j)], back.at[c, :, lane_rows(y, cap)],
                made_send.at[m, j - 1], made_recv.at[m, j - 1], {"expert": z * lanes + lane_peer(j)},
            )
            for j in range(1, lanes)
        ])
        own_part, mate_part = pl.ds(0, half), pl.ds(half, half)
        backs.append([
            remote(back.at[c, 1, own_part], back.at[c, 0, mate_part], back_send.at[m, 0], back_recv.at[m, 0], mate),
            remote(
                back.at[c, pl.ds(2, 2), own_part], back.at[c, pl.ds(2, 2), mate_part],
                back_send.at[m, 1], back_recv.at[m, 1], mate,
            ),
        ])
        parts.append(remote(part_out.at[c], part_in.at[c], part_send.at[m], part_recv.at[m], far))
        fins.append(remote(fin_out.at[c], part_in.at[c, 0], fin_send.at[m], fin_recv.at[m], mate))
        target = (layer_out, tokens_grad)[m // chunks]
        outs.append(pltpu.make_async_copy(out_stage.at[m % 4], target.at[:, columns(m)], out_sem.at[m]))
    info_onward = remote(info.at[0], info.at[onward_slot], info_send.at[0], info_recv.at[onward_slot], onward)
    info_forward = remote(info.at[1], info.at[3], info_send.at[1], info_recv.at[3], far)
    info_from_mate = remote(info.at[1], info.at[1], info_send.at[0], info_recv.at[1], mate)
    info_from_far = remote(info.at[2], info.at[2], info_send.at[0], info_recv.at[2], far)

    group_copies = []

    def to_group(source, target, shift, send, recv):
        if shift == 0:
            copy = pltpu.make_async_copy(source, target, send)
        else:
            copy = remote(source, target, send, recv, group_peer(shift))
        copy.start()
        group_copies.append((shift, copy))

    for n in range(2):
        loads[n].start()
    for u in range(ring):
        for load in weight_loads(u):
            load.start()
    barrier = pltpu.get_barrier_semaphore()
    for shift in range(1, groups):
        pl.semaphore_signal(barrier, inc=1, device_id=group_peer(shift))
    for j in range(1, lanes):
        pl.semaphore_signal(barrier, inc=1, device_id={"expert": z * lanes + lane_peer(j)})
    pl.semaphore_signal(barrier, inc=1, device_id=mate)

    @pl.when(inner)
    def _():
        pl.semaphore_signal(barrier, inc=1, device_id=far)
        pl.semaphore_wait(barrier, lanes + groups)

    @pl.when(outer)
    def _():
        pl.semaphore_wait(barrier, lanes + groups - 1)

    onwards[0].start()
    onwards[1].start()

    expert_range = lax.broadcasted_iota(jnp.int32, (experts, tok_count), 0)
    named = [ids[k : k + 1, :] == expert_range for k in range(2)]
    chosen = jnp.where(named[0], 1.0, 0.0) + jnp.where(named[1], 1.0, 0.0)
    before = lax.broadcasted_iota(jnp.int32, (tok_count, tok_count), 0)
    after = lax.broadcasted_iota(jnp.int32, (tok_count, tok_count), 1)
    earlier = jnp.where(before < after, 1.0, 0.0).astype(BF16)
    ranks = jnp.dot(chosen.astype(BF16), earlier, preferred_element_type=F32)
    info[0, 0:experts] = jnp.where(chosen > 0.5, ranks, -1.0)
    gates = [jnp.where(named[k], codes[k : k + 1, :].astype(F32), 0.0) for k in range(2)]
    info[0, experts : 2 * experts] = (gates[0] + gates[1]) * (1.0 / 64.0)
    info_onward.start()
    for q in range(chunks):
        down_load(q).start()

    slot_range = lax.broadcasted_iota(jnp.int32, (cap, tok_count), 0).astype(F32)
    diagonal = jnp.where(before == after, 1.0, 0.0).astype(BF16)

    def select(s, planes_used):
        for p in range(planes_used):
            for lane in range(lanes):
                expert = (z, mate_z)[p] * lanes + lane
                hit = info[s, pl.ds(expert, 1), :] == slot_range
                gate = info[s, pl.ds(experts + expert, 1), :]
                at = pl.ds(p * half + lane * cap, cap)
                sel[0, s, at] = jnp.where(hit, 1.0, 0.0).astype(BF16)
                sel[1, s, at] = jnp.where(hit, gate, 0.0).astype(BF16)
        for kind in range(2):
            matrix = sel[kind, s, 0 : planes_used * half]
            turned = lax.dot_general(diagonal, matrix, CONTRACT, preferred_element_type=F32).astype(BF16)
            if planes_used == 2:
                selt[kind, s] = turned
            else:
                half_selt[kind] = turned

    @pl.when(inner)
    def _():
        select(0, 2)
        info_from_mate.wait_recv()
        info_forward.start()
        select(1, 1)
        info_from_far.wait_recv()
        select(2, 2)
        info_forward.wait_recv()
        select(3, 2)
        info_forward.wait_send()

    @pl.when(outer)
    def _():
        select(0, 1)

    info_onward.wait_send()

    def spread(n, s, start, count):
        kind = n // chunks
        values = jnp.dot(
            sel[kind, s, start : start + count], raw[s, n % chunks], preferred_element_type=F32
        )
        return values.astype(BF16)

    def into_plane(n, s, values):
        for lane in range(lanes):
            plane[n % chunks, lane, s * cap : (s + 1) * cap] = values[lane * cap : (lane + 1) * cap]

    def keep_own(n):
        for copy in planes[n]:
            copy.start()
        landed[n, lane_rows(y, quad)] = plane[n % chunks, y]

    def stage_forward(n):
        @pl.when(inner)
        def _():
            from_mate_raw[n].wait_recv()
            forwards[n].start()

    def stage_spread(n):
        c = n % chunks
        loads[n].wait()

        @pl.when(inner)
        def _():
            if n >= 1:
                forwards[n - 1].wait_send()
            if n >= chunks:
                mates[n - chunks].wait_send()
            both = spread(n, 0, 0, 2 * half)
            into_plane(n, 0, both[:half])
            mine = [both[half:]]
            into_plane(n, 1, spread(n, 1, 0, half))
            from_far_raw[n].wait_recv()
            both = spread(n, 2, 0, 2 * half)
            into_plane(n, 2, both[:half])
            mine.append(both[half:])
            forwards[n].wait_recv()
            both = spread(n, 3, 0, 2 * half)
            into_plane(n, 3, both[:half])
            mine.append(both[half:])
            for k in range(3):
                for lane in range(lanes):
                    mate_stage[c, lane, k * cap : (k + 1) * cap] = mine[k][lane * cap : (lane + 1) * cap]
            mates[n].start()
            keep_own(n)

        @pl.when(outer)
        def _():
            into_plane(n, 0, spread(n, 0, 0, half))

    def stage_relay(n):
        @pl.when(outer)
        def _():
            mates[n].wait_recv()
            keep_own(n)

    def stage_multiply(n):
        q = n % chunks
        for copy in planes[n]:
            copy.wait_recv()
        shift, inside = place(n)
        target = (token_cols, grad_cols)[n // chunks]
        to_group(
            landed.at[n], target.at[shift, :, pl.ds(inside * width, width)], shift, group_send.at[n], group_recv.at[n]
        )
        rows = landed[n]
        if n < chunks:
            for load in weight_loads(n):
                load.wait()
            for total, matrix in ((pre_gate, vgate), (pre_up, vup)):
                term = jnp.dot(rows, matrix[n % ring], preferred_element_type=F32)
                total[...] = term if q == 0 else total[...] + term
            for load in weight_loads(n + ring):
                load.start()
            if q == chunks - 1:
                for start in range(0, pre_gate.shape[0], cap):
                    at = pl.ds(start, cap)
                    gate = pre_gate[at, :]
                    hidden[at, :] = (gate * jax.nn.sigmoid(gate) * pre_up[at, :]).astype(BF16)
                send_act(0, hidden, all_hidden)
        else:
            if n == chunks:
                for p in range(chunks):
                    down_load(p).wait()
            term = lax.dot_general(rows, vdown[q], CONTRACT, preferred_element_type=F32)
            hidden_grad[...] = term if q == 0 else hidden_grad[...] + term
            if q == chunks - 1:
                for start in range(0, pre_gate.shape[0], cap):
                    at = pl.ds(start, cap)
                    gate, up, grad = pre_gate[at, :], pre_up[at, :], hidden_grad[at, :]
                    sigmoid = jax.nn.sigmoid(gate)
                    silu = gate * sigmoid
                    gate_pre[at, :] = (grad * up * sigmoid * (1.0 + gate * (1.0 - sigmoid))).astype(BF16)
                    up_pre[at, :] = (grad * silu).astype(BF16)
                send_act(1, gate_pre, all_gate)
                send_act(2, up_pre, all_up)

    def send_act(kind, source, target):
        for order in range(groups):
            shift = (order + 1) % groups
            to_group(source, target.at[shift], shift, act_send.at[kind, shift], act_recv.at[kind, shift])

    def stage_make(m):
        c = m % chunks
        if m < chunks:
            values = jnp.dot(hidden[...], vdown[c], preferred_element_type=F32)
        else:
            slot = m % ring
            for load in weight_loads(m):
                load.wait()
            values = lax.dot_general(gate_pre[...], vgate[slot], CONTRACT, preferred_element_type=F32)
            values = values + lax.dot_general(up_pre[...], vup[slot], CONTRACT, preferred_element_type=F32)
            if m + ring < pieces:
                for load in weight_loads(m + ring):
                    load.start()
            for copy in mades[m - chunks]:
                copy.wait_send()
        made[c] = values.astype(BF16).reshape(lanes, LINE, cap, width)
        for copy in mades[m]:
            copy.start()
        back[c, :, lane_rows(y, cap)] = made[c, y]

    def stage_hand(m):
        @pl.when(outer)
        def _():
            for copy in mades[m]:
                copy.wait_recv()
            for copy in backs[m]:
                copy.start()

    def gather(m, s):
        kind = 1 - m // chunks
        return jnp.dot(selt[kind, s], back[m % chunks, s], preferred_element_type=F32)

    def gather_half(m, s):
        kind = 1 - m // chunks
        return jnp.dot(half_selt[kind], back[m % chunks, s, 0:half], preferred_element_type=F32)

    def stage_partial(m):
        c = m % chunks

        @pl.when(inner)
        def _():
            for copy in mades[m]:
                copy.wait_recv()
            for copy in backs[m]:
                copy.wait_recv()
            if m >= chunks:
                parts[m - chunks].wait_send()
            for s in (2, 3):
                part_out[c, s - 2] = gather(m, s).astype(BF16)
            parts[m].start()

    def stage_finish(m):
        c = m % chunks
        if m >= 4:
            outs[m - 4].wait()

        @pl.when(inner)
        def _():
            if m >= chunks:
                fins[m - chunks].wait_send()
            near = gather_half(m, 1)
            own = gather(m, 0)
            parts[m].wait_recv()
            fin_out[c] = (near + part_in[c, 1].astype(F32)).astype(BF16)
            fins[m].start()
            out_stage[m % 4] = (own + part_in[c, 0].astype(F32)).astype(BF16)

        @pl.when(outer)
        def _():
            near = gather_half(m, 0)
            for copy in backs[m]:
                copy.wait_send()
            fins[m].wait_recv()
            out_stage[m % 4] = (near + part_in[c, 0].astype(F32)).astype(BF16)

        outs[m].start()

    stage_forward(0)
    first_make = chunks + 2
    for tick in range(first_make + pieces + 3):
        n = tick + 2
        if n < pieces:
            if n >= chunks:
                for copy in planes[n - chunks]:
                    copy.wait_send()
            loads[n].start()
            onwards[n].start()
        m = tick - first_make
        if 0 <= m - 1 < pieces:
            stage_hand(m - 1)
        if 0 <= m - 2 < pieces:
            stage_partial(m - 2)
        if tick + 1 < pieces:
            stage_forward(tick + 1)
        if tick < pieces:
            stage_spread(tick)
        if 0 <= tick - 1 < pieces:
            stage_relay(tick - 1)
        if 0 <= tick - 2 < pieces:
            stage_multiply(tick - 2)
        if 0 <= m < pieces:
            stage_make(m)
        if 0 <= m - 3 < pieces:
            stage_finish(m - 3)

    for n in range(pieces):
        onwards[n].wait_send()
    for n in range(chunks, pieces):
        for copy in planes[n]:
            copy.wait_send()
    for m in range(chunks, pieces):
        for copy in mades[m]:
            copy.wait_send()
    for m in range(pieces - 4, pieces):
        outs[m].wait()

    @pl.when(inner)
    def _():
        forwards[pieces - 1].wait_send()
        for n in range(chunks, pieces):
            mates[n].wait_send()
        for m in range(chunks, pieces):
            parts[m].wait_send()
            fins[m].wait_send()

    for shift, copy in group_copies:
        if shift == 0:
            copy.wait()
        else:
            copy.wait_recv()
            copy.wait_send()


def weights_kernel(
    layer_in, tokens_in, token_cols, grad_cols, all_hidden, all_gate, all_up,
    layer_out, tokens_grad, gate_sum, up_sum, down_sum,
    left, grads, acts, moved, result, load_sem, move_sem, out_sem,
):
    through = ((layer_in, layer_out), (tokens_in, tokens_grad))
    moves = [pltpu.make_async_copy(a, moved.at[i], move_sem.at[i]) for i, (a, _) in enumerate(through)]
    moves_out = [pltpu.make_async_copy(moved.at[i], b, move_sem.at[2 + i]) for i, (_, b) in enumerate(through)]
    pairs = (
        (all_hidden, acts.at[0]), (grad_cols, grads), (token_cols, left), (all_gate, acts.at[1]), (all_up, acts.at[2])
    )
    loads = [pltpu.make_async_copy(a, b, load_sem.at[i]) for i, (a, b) in enumerate(pairs)]
    for copy in loads + moves:
        copy.start()
    depth = left.shape[0] * left.shape[1]
    block = left.shape[2]
    units = acts.shape[3]
    tile = 256
    stores = []

    def matrix(ref, at):
        return ref[:, :, at].reshape(depth, at.size)

    def put(values, target):
        i = len(stores)
        slot = i % 2
        if i >= 2:
            stores[i - 2].wait()
        result[slot, :, 0 : values.shape[1]] = values.astype(BF16)
        copy = pltpu.make_async_copy(result.at[slot, :, pl.ds(0, values.shape[1])], target, out_sem.at[i])
        copy.start()
        stores.append(copy)

    loads[0].wait()
    loads[1].wait()
    for start in range(0, units, tile):
        at = pl.ds(start, tile)
        values = lax.dot_general(
            matrix(acts.at[0], at), matrix(grads, pl.ds(0, block)), ROWS_FIRST, preferred_element_type=F32
        )
        put(values, down_sum.at[at, :])
    for copy, copy_out in zip(moves, moves_out):
        copy.wait()
        copy_out.start()
    loads[2].wait()
    for kind, target in ((1, gate_sum), (2, up_sum)):
        loads[2 + kind].wait()
        for start in range(0, block, tile):
            at = pl.ds(start, tile)
            values = lax.dot_general(
                matrix(left, at), matrix(acts.at[kind], pl.ds(0, units)), ROWS_FIRST, preferred_element_type=F32
            )
            put(values, target.at[at, :])
    for copy in stores[-2:] + moves_out:
        copy.wait()


def per_device(tokens, expert_ids, gate_codes, w_gate, w_up, w_down, out_grad):
    experts = lax.axis_size("expert")
    groups = lax.axis_size("dp")
    lanes = experts // LINE
    tok_count, model_width = tokens.shape
    pair_count = tok_count * expert_ids.shape[1]
    capacity = 3 * pair_count // (2 * experts)
    capacity = -(-capacity // 16) * 16
    rows = experts * capacity
    half = lanes * capacity
    chunks = groups * max(1, 8 // groups)
    ring = chunks // 2
    width = model_width // chunks
    block = model_width // groups
    pieces = 2 * chunks
    gate_matrix, up_matrix, down_matrix = w_gate[0], w_up[0], w_down[0]
    units = gate_matrix.shape[1]
    vmem = pl.BlockSpec(memory_space=pltpu.VMEM)
    anywhere = pl.BlockSpec(memory_space=pl.ANY)
    dma = pltpu.SemaphoreType.DMA

    def shape(*dims):
        return jax.ShapeDtypeStruct(dims, BF16)

    def buffer(*dims):
        return pltpu.VMEM(dims, BF16)

    peers = max(1, lanes - 1)
    layer_out, tokens_grad, *factors = pl.pallas_call(
        functools.partial(exchange_kernel, lanes, capacity, groups, chunks, ring),
        out_shape=(
            shape(tok_count, model_width),
            shape(tok_count, model_width),
            shape(groups, rows, block),
            shape(groups, rows, block),
            shape(groups, rows, units),
            shape(groups, rows, units),
            shape(groups, rows, units),
        ),
        in_specs=[vmem] * 2 + [anywhere] * 5,
        out_specs=(anywhere,) * 7,
        scratch_shapes=[
            pltpu.VMEM((LINE, 2 * experts, tok_count), F32),
            buffer(LINE, chunks, tok_count, width),
            buffer(2, LINE, 2 * half, tok_count),
            buffer(2, LINE, tok_count, 2 * half),
            buffer(2, tok_count, half),
            buffer(chunks, lanes, LINE * capacity, width),
            buffer(chunks, lanes, 3 * capacity, width),
            buffer(pieces, rows, width),
            pltpu.VMEM((rows, units), F32),
            pltpu.VMEM((rows, units), F32),
            pltpu.VMEM((rows, units), F32),
            buffer(rows, units),
            buffer(rows, units),
            buffer(rows, units),
            buffer(chunks, units, width),
            buffer(ring, width, units),
            buffer(ring, width, units),
            buffer(chunks, lanes, LINE, capacity, width),
            buffer(chunks, LINE, 2 * half, width),
            buffer(chunks, 2, tok_count, width),
            buffer(chunks, 2, tok_count, width),
            buffer(chunks, tok_count, width),
            buffer(4, tok_count, width),
            dma((2,)),
            dma((LINE,)),
            dma((pieces,)),
            dma((pieces,)),
            dma((pieces, LINE)),
            dma((pieces,)),
            dma((pieces, peers)),
            dma((pieces, peers)),
            dma((pieces,)),
            dma((pieces,)),
            dma((pieces, peers)),
            dma((pieces, peers)),
            dma((pieces, 2)),
            dma((pieces, 2)),
            dma((pieces,)),
            dma((pieces,)),
            dma((pieces,)),
            dma((pieces,)),
            dma((pieces,)),
            dma((pieces, 2)),
            dma((chunks,)),
            dma((pieces,)),
            dma((pieces,)),
            dma((3, groups)),
            dma((3, groups)),
        ],
        compiler_params=pltpu.CompilerParams(
            collective_id=0, has_side_effects=True, vmem_limit_bytes=63 * MIB
        ),
    )(expert_ids.T, gate_codes.T, tokens, out_grad, gate_matrix, up_matrix, down_matrix)

    outs = pl.pallas_call(
        weights_kernel,
        out_shape=(
            shape(tok_count, model_width),
            shape(tok_count, model_width),
            shape(block, units),
            shape(block, units),
            shape(units, block),
        ),
        in_specs=[anywhere] * 7,
        out_specs=(anywhere,) * 5,
        scratch_shapes=[
            buffer(groups, rows, block),
            buffer(groups, rows, block),
            buffer(3, groups, rows, units),
            buffer(2, tok_count, model_width),
            buffer(2, 256, max(block, units)),
            dma((5,)),
            dma((4,)),
            dma((units // 256 + 2 * (block // 256),)),
        ],
        compiler_params=pltpu.CompilerParams(vmem_limit_bytes=56 * MIB),
    )(layer_out, tokens_grad, *factors)
    layer_out, tokens_grad, gate_sum, up_sum, down_sum = outs
    return layer_out, tokens_grad, gate_sum[None], up_sum[None], down_sum[None]


def solution(mesh):
    placed = (
        P(("dp", "expert"), None),
        P(("dp", "expert"), None),
        P(("dp", "expert"), None),
        P("expert", None, None),
        P("expert", None, None),
        P("expert", None, None),
        P(("dp", "expert"), None),
    )
    return jax.shard_map(
        per_device,
        mesh=mesh,
        in_specs=placed,
        out_specs=(
            P(("dp", "expert"), None),
            P(("dp", "expert"), None),
            P("expert", "dp", None),
            P("expert", "dp", None),
            P("expert", None, "dp"),
        ),
        check_vma=False,
    )
```

```python
import functools

import jax
import jax.numpy as jnp
from jax import lax
from jax.experimental import pallas as pl
from jax.experimental.pallas import tpu as pltpu
from jax.sharding import PartitionSpec as P

F32 = jnp.float32
BF16 = jnp.bfloat16
CONTRACT = (((1,), (1,)), ((), ()))
ROWS_FIRST = (((0,), (0,)), ((), ()))
LINE = 4
PIECES = 16
DEEP = (2, 1, 2, 4, 2, 4, 6, 8)
SHALLOW = (2, 1, 1, 2, 1, 2, 3, 3)
MIB = 2**20


def remote(src, dst, send, recv, peer):
    return pltpu.make_async_remote_copy(src_ref=src, dst_ref=dst, send_sem=send, recv_sem=recv, device_id=peer)


def exchange_kernel(
    lanes, cap, groups, chunks, ring, slots, lags,
    ids, codes, tokens, out_grad, w_gate, w_up, w_down,
    layer_out, tokens_grad, token_cols, grad_cols, all_hidden, all_gate, all_up,
    info, raw, sel, selt, half_selt, plane, mate_stage, landed, pre_gate, pre_up, hidden_grad,
    hidden, gate_pre, up_pre, vdown, vgate, vup, made, back, part_out, part_in, fin_out, out_stage,
    info_send, info_recv, raw_load, raw_send, raw_recv, forward_send, plane_send, plane_recv,
    mate_send, mate_recv, made_send, made_recv, back_send, back_recv, part_send, part_recv,
    fin_send, fin_recv, out_sem, weight_sem, down_sem, group_send, group_recv, act_send, act_recv,
):
    me = lax.axis_index("expert")
    group = lax.axis_index("dp")
    z = me // lanes
    y = me - z * lanes
    inner = (z + 1) // 2 == 1
    outer = (z + 1) // 2 != 1
    mate_z = z + 1 - 2 * lax.rem(z, 2)
    far_z = LINE - 1 - z
    mate = {"expert": mate_z * lanes + y}
    far = {"expert": far_z * lanes + y}
    onward = {"expert": jnp.where(inner, far_z, mate_z) * lanes + y}
    onward_slot = jnp.where(inner, 2, 1)
    experts = LINE * lanes
    tok_count, model_width = tokens.shape
    width = model_width // chunks
    block = model_width // groups
    per_block = chunks // groups
    pieces = 2 * chunks
    half = lanes * cap
    quad = LINE * cap
    sources = (tokens, out_grad)

    def lane_peer(j):
        return lax.rem(y + j, lanes)

    def group_peer(shift):
        return {"dp": lax.rem(group + shift, groups)}

    def place(n):
        order, inside = divmod(n % chunks, per_block)
        return (order + 1) % groups, inside

    def columns(n):
        shift, inside = place(n)
        start = lax.rem(group + shift, groups) * block + inside * width
        return pl.ds(pl.multiple_of(start, 128), width)

    def lane_rows(index, count):
        return pl.ds(pl.multiple_of(index * count, 16), count)

    def weight_loads(u):
        at, slot = columns(u), u % ring
        return (
            pltpu.make_async_copy(w_gate.at[at, :], vgate.at[slot], weight_sem.at[u, 0]),
            pltpu.make_async_copy(w_up.at[at, :], vup.at[slot], weight_sem.at[u, 1]),
        )

    def down_load(q):
        return pltpu.make_async_copy(w_down.at[:, columns(q)], vdown.at[q], down_sem.at[q])

    loads, onwards, forwards, mates, planes = [], [], [], [], []
    from_mate_raw, from_far_raw = [], []
    for n in range(pieces):
        c = n % chunks
        source = sources[n // chunks].at[:, columns(n)]
        loads.append(pltpu.make_async_copy(source, raw.at[0, c], raw_load.at[n]))
        onwards.append(remote(source, raw.at[onward_slot, c], raw_send.at[n], raw_recv.at[n, onward_slot], onward))
        forwards.append(remote(raw.at[1, c], raw.at[3, c], forward_send.at[n], raw_recv.at[n, 3], far))
        from_mate_raw.append(remote(raw.at[1, c], raw.at[1, c], raw_send.at[n], raw_recv.at[n, 1], mate))
        from_far_raw.append(remote(raw.at[2, c], raw.at[2, c], raw_send.at[n], raw_recv.at[n, 2], far))
        mates.append(
            remote(mate_stage.at[c], plane.at[c, :, pl.ds(cap, 3 * cap)], mate_send.at[n], mate_recv.at[n], mate)
        )
        planes.append([
            remote(
                plane.at[c, lane_peer(j)], landed.at[n, lane_rows(y, quad)],
                plane_send.at[n, j - 1], plane_recv.at[n, j - 1], {"expert": z * lanes + lane_peer(j)},
            )
            for j in range(1, lanes)
        ])
    mades, backs, parts, fins, outs = [], [], [], [], []
    for m in range(pieces):
        c, b = m % chunks, m % slots
        mades.append([
            remote(
                made.at[c, lane_peer(j)], back.at[b, :, lane_rows(y, cap)],
                made_send.at[m, j - 1], made_recv.at[m, j - 1], {"expert": z * lanes + lane_peer(j)},
            )
            for j in range(1, lanes)
        ])
        own_part, mate_part = pl.ds(0, half), pl.ds(half, half)
        backs.append([
            remote(back.at[b, 1, own_part], back.at[b, 0, mate_part], back_send.at[m, 0], back_recv.at[m, 0], mate),
            remote(
                back.at[b, pl.ds(2, 2), own_part], back.at[b, pl.ds(2, 2), mate_part],
                back_send.at[m, 1], back_recv.at[m, 1], mate,
            ),
        ])
        parts.append(remote(part_out.at[c], part_in.at[b], part_send.at[m], part_recv.at[m], far))
        fins.append(remote(fin_out.at[c], part_in.at[b, 0], fin_send.at[m], fin_recv.at[m], mate))
        target = (layer_out, tokens_grad)[m // chunks]
        outs.append(pltpu.make_async_copy(out_stage.at[m % 4], target.at[:, columns(m)], out_sem.at[m]))
    info_onward = remote(info.at[0], info.at[onward_slot], info_send.at[0], info_recv.at[onward_slot], onward)
    info_forward = remote(info.at[1], info.at[3], info_send.at[1], info_recv.at[3], far)
    info_from_mate = remote(info.at[1], info.at[1], info_send.at[0], info_recv.at[1], mate)
    info_from_far = remote(info.at[2], info.at[2], info_send.at[0], info_recv.at[2], far)

    group_copies = []

    def to_group(source, target, shift, send, recv):
        if shift == 0:
            copy = pltpu.make_async_copy(source, target, send)
        else:
            copy = remote(source, target, send, recv, group_peer(shift))
        copy.start()
        group_copies.append((shift, copy))

    lead = lags[0]
    for n in range(lead):
        loads[n].start()
    for u in range(ring):
        for load in weight_loads(u):
            load.start()
    barrier = pltpu.get_barrier_semaphore()
    for shift in range(1, groups):
        pl.semaphore_signal(barrier, inc=1, device_id=group_peer(shift))
    for j in range(1, lanes):
        pl.semaphore_signal(barrier, inc=1, device_id={"expert": z * lanes + lane_peer(j)})
    pl.semaphore_signal(barrier, inc=1, device_id=mate)

    @pl.when(inner)
    def _():
        pl.semaphore_signal(barrier, inc=1, device_id=far)
        pl.semaphore_wait(barrier, lanes + groups)

    @pl.when(outer)
    def _():
        pl.semaphore_wait(barrier, lanes + groups - 1)

    for n in range(lead):
        onwards[n].start()

    expert_range = lax.broadcasted_iota(jnp.int32, (experts, tok_count), 0)
    named = [ids[k : k + 1, :] == expert_range for k in range(2)]
    chosen = jnp.where(named[0], 1.0, 0.0) + jnp.where(named[1], 1.0, 0.0)
    before = lax.broadcasted_iota(jnp.int32, (tok_count, tok_count), 0)
    after = lax.broadcasted_iota(jnp.int32, (tok_count, tok_count), 1)
    earlier = jnp.where(before < after, 1.0, 0.0).astype(BF16)
    ranks = jnp.dot(chosen.astype(BF16), earlier, preferred_element_type=F32)
    info[0, 0:experts] = jnp.where(chosen > 0.5, ranks, -1.0)
    gates = [jnp.where(named[k], codes[k : k + 1, :].astype(F32), 0.0) for k in range(2)]
    info[0, experts : 2 * experts] = (gates[0] + gates[1]) * (1.0 / 64.0)
    info_onward.start()
    for q in range(chunks):
        down_load(q).start()

    slot_range = lax.broadcasted_iota(jnp.int32, (cap, tok_count), 0).astype(F32)
    diagonal = jnp.where(before == after, 1.0, 0.0).astype(BF16)

    def select(s, planes_used):
        for p in range(planes_used):
            for lane in range(lanes):
                expert = (z, mate_z)[p] * lanes + lane
                hit = info[s, pl.ds(expert, 1), :] == slot_range
                gate = info[s, pl.ds(experts + expert, 1), :]
                at = pl.ds(p * half + lane * cap, cap)
                sel[0, s, at] = jnp.where(hit, 1.0, 0.0).astype(BF16)
                sel[1, s, at] = jnp.where(hit, gate, 0.0).astype(BF16)
        for kind in range(2):
            matrix = sel[kind, s, 0 : planes_used * half]
            turned = lax.dot_general(diagonal, matrix, CONTRACT, preferred_element_type=F32).astype(BF16)
            if planes_used == 2:
                selt[kind, s] = turned
            else:
                half_selt[kind] = turned

    @pl.when(inner)
    def _():
        select(0, 2)
        info_from_mate.wait_recv()
        info_forward.start()
        select(1, 1)
        info_from_far.wait_recv()
        select(2, 2)
        info_forward.wait_recv()
        select(3, 2)
        info_forward.wait_send()

    @pl.when(outer)
    def _():
        select(0, 1)

    info_onward.wait_send()

    def spread(n, s, start, count):
        kind = n // chunks
        values = jnp.dot(
            sel[kind, s, start : start + count], raw[s, n % chunks], preferred_element_type=F32
        )
        return values.astype(BF16)

    def into_plane(n, s, values):
        for lane in range(lanes):
            plane[n % chunks, lane, s * cap : (s + 1) * cap] = values[lane * cap : (lane + 1) * cap]

    def keep_own(n):
        for copy in planes[n]:
            copy.start()
        landed[n, lane_rows(y, quad)] = plane[n % chunks, y]

    def stage_forward(n):
        @pl.when(inner)
        def _():
            from_mate_raw[n].wait_recv()
            forwards[n].start()

    def stage_spread(n):
        c = n % chunks
        loads[n].wait()

        @pl.when(inner)
        def _():
            if n >= 1:
                forwards[n - 1].wait_send()
            if n >= chunks:
                mates[n - chunks].wait_send()
            both = spread(n, 0, 0, 2 * half)
            into_plane(n, 0, both[:half])
            mine = [both[half:]]
            into_plane(n, 1, spread(n, 1, 0, half))
            from_far_raw[n].wait_recv()
            both = spread(n, 2, 0, 2 * half)
            into_plane(n, 2, both[:half])
            mine.append(both[half:])
            forwards[n].wait_recv()
            both = spread(n, 3, 0, 2 * half)
            into_plane(n, 3, both[:half])
            mine.append(both[half:])
            for k in range(3):
                for lane in range(lanes):
                    mate_stage[c, lane, k * cap : (k + 1) * cap] = mine[k][lane * cap : (lane + 1) * cap]
            mates[n].start()
            keep_own(n)

        @pl.when(outer)
        def _():
            into_plane(n, 0, spread(n, 0, 0, half))

    def stage_relay(n):
        @pl.when(outer)
        def _():
            mates[n].wait_recv()
            keep_own(n)

    def stage_multiply(n):
        q = n % chunks
        for copy in planes[n]:
            copy.wait_recv()
        shift, inside = place(n)
        target = (token_cols, grad_cols)[n // chunks]
        to_group(
            landed.at[n], target.at[shift, :, pl.ds(inside * width, width)], shift, group_send.at[n], group_recv.at[n]
        )
        rows = landed[n]
        if n < chunks:
            for load in weight_loads(n):
                load.wait()
            for total, matrix in ((pre_gate, vgate), (pre_up, vup)):
                term = jnp.dot(rows, matrix[n % ring], preferred_element_type=F32)
                total[...] = term if q == 0 else total[...] + term
            for load in weight_loads(n + ring):
                load.start()
            if q == chunks - 1:
                for p in range(chunks):
                    down_load(p).wait()
                for start in range(0, pre_gate.shape[0], cap):
                    at = pl.ds(start, cap)
                    gate = pre_gate[at, :]
                    hidden[at, :] = (gate * jax.nn.sigmoid(gate) * pre_up[at, :]).astype(BF16)
                send_act(0, hidden, all_hidden)
        else:
            term = lax.dot_general(rows, vdown[q], CONTRACT, preferred_element_type=F32)
            hidden_grad[...] = term if q == 0 else hidden_grad[...] + term
            if q == chunks - 1:
                for start in range(0, pre_gate.shape[0], cap):
                    at = pl.ds(start, cap)
                    gate, up, grad = pre_gate[at, :], pre_up[at, :], hidden_grad[at, :]
                    sigmoid = jax.nn.sigmoid(gate)
                    silu = gate * sigmoid
                    gate_pre[at, :] = (grad * up * sigmoid * (1.0 + gate * (1.0 - sigmoid))).astype(BF16)
                    up_pre[at, :] = (grad * silu).astype(BF16)
                send_act(1, gate_pre, all_gate)
                send_act(2, up_pre, all_up)

    def send_act(kind, source, target):
        for order in range(groups):
            shift = (order + 1) % groups
            to_group(source, target.at[shift], shift, act_send.at[kind, shift], act_recv.at[kind, shift])

    def stage_make(m):
        c = m % chunks
        if m < chunks:
            values = jnp.dot(hidden[...], vdown[c], preferred_element_type=F32)
        else:
            slot = m % ring
            for load in weight_loads(m):
                load.wait()
            values = lax.dot_general(gate_pre[...], vgate[slot], CONTRACT, preferred_element_type=F32)
            values = values + lax.dot_general(up_pre[...], vup[slot], CONTRACT, preferred_element_type=F32)
            if m + ring < pieces:
                for load in weight_loads(m + ring):
                    load.start()
            for copy in mades[m - chunks]:
                copy.wait_send()
        made[c] = values.astype(BF16).reshape(lanes, LINE, cap, width)
        for copy in mades[m]:
            copy.start()
        back[m % slots, :, lane_rows(y, cap)] = made[c, y]

    def stage_hand(m):
        @pl.when(outer)
        def _():
            for copy in mades[m]:
                copy.wait_recv()
            for copy in backs[m]:
                copy.start()

    def gather(m, s):
        kind = 1 - m // chunks
        return jnp.dot(selt[kind, s], back[m % slots, s], preferred_element_type=F32)

    def gather_half(m, s):
        kind = 1 - m // chunks
        return jnp.dot(half_selt[kind], back[m % slots, s, 0:half], preferred_element_type=F32)

    def stage_partial(m):
        c = m % chunks

        @pl.when(inner)
        def _():
            for copy in mades[m]:
                copy.wait_recv()
            for copy in backs[m]:
                copy.wait_recv()
            if m >= chunks:
                parts[m - chunks].wait_send()
            for s in (2, 3):
                part_out[c, s - 2] = gather(m, s).astype(BF16)
            parts[m].start()

    def put_out(m, values):
        if m >= 4:
            outs[m - 4].wait()
        out_stage[m % 4] = values.astype(BF16)
        outs[m].start()

    def stage_finish_inner(m):
        c, b = m % chunks, m % slots

        @pl.when(inner)
        def _():
            if m >= chunks:
                fins[m - chunks].wait_send()
            near = gather_half(m, 1)
            own = gather(m, 0)
            parts[m].wait_recv()
            fin_out[c] = (near + part_in[b, 1].astype(F32)).astype(BF16)
            fins[m].start()
            put_out(m, own + part_in[b, 0].astype(F32))

    def stage_finish_outer(m):
        @pl.when(outer)
        def _():
            near = gather_half(m, 0)
            for copy in backs[m]:
                copy.wait_send()
            fins[m].wait_recv()
            put_out(m, near + part_in[m % slots, 0].astype(F32))

    _, ahead, relay, multiply, hand, partial, finish_inner, finish_outer = lags
    first_make = chunks + multiply
    stages = (
        (-ahead, stage_forward),
        (first_make + partial, stage_partial),
        (0, stage_spread),
        (first_make + hand, stage_hand),
        (relay, stage_relay),
        (first_make, stage_make),
        (multiply, stage_multiply),
        (first_make + finish_inner, stage_finish_inner),
        (first_make + finish_outer, stage_finish_outer),
    )
    for n in range(ahead):
        stage_forward(n)
    for tick in range(first_make + pieces + finish_outer):
        n = tick + lead
        if n < pieces:
            if n >= chunks:
                for copy in planes[n - chunks]:
                    copy.wait_send()
            loads[n].start()
            onwards[n].start()
        for lag, stage in stages:
            n = tick - lag
            if 0 <= n < pieces and (stage is not stage_forward or n >= ahead):
                stage(n)

    for n in range(pieces):
        onwards[n].wait_send()
    for n in range(chunks, pieces):
        for copy in planes[n]:
            copy.wait_send()
    for m in range(chunks, pieces):
        for copy in mades[m]:
            copy.wait_send()
    for m in range(pieces - 4, pieces):
        outs[m].wait()

    @pl.when(inner)
    def _():
        forwards[pieces - 1].wait_send()
        for n in range(chunks, pieces):
            mates[n].wait_send()
        for m in range(chunks, pieces):
            parts[m].wait_send()
            fins[m].wait_send()

    for shift, copy in group_copies:
        if shift == 0:
            copy.wait()
        else:
            copy.wait_recv()
            copy.wait_send()


def weights_kernel(
    layer_in, tokens_in, token_cols, grad_cols, all_hidden, all_gate, all_up,
    layer_out, tokens_grad, gate_sum, up_sum, down_sum,
    left, grads, acts, moved, result, load_sem, move_sem, out_sem,
):
    through = ((layer_in, layer_out), (tokens_in, tokens_grad))
    moves = [pltpu.make_async_copy(a, moved.at[i], move_sem.at[i]) for i, (a, _) in enumerate(through)]
    moves_out = [pltpu.make_async_copy(moved.at[i], b, move_sem.at[2 + i]) for i, (_, b) in enumerate(through)]
    pairs = (
        (all_hidden, acts.at[0]), (grad_cols, grads), (token_cols, left), (all_gate, acts.at[1]), (all_up, acts.at[2])
    )
    loads = [pltpu.make_async_copy(a, b, load_sem.at[i]) for i, (a, b) in enumerate(pairs)]
    for copy in loads + moves:
        copy.start()
    depth = left.shape[0] * left.shape[1]
    block = left.shape[2]
    units = acts.shape[3]
    tile = 256
    stores = []

    def matrix(ref, at):
        return ref[:, :, at].reshape(depth, at.size)

    def put(values, target):
        i = len(stores)
        slot = i % 2
        if i >= 2:
            stores[i - 2].wait()
        result[slot, :, 0 : values.shape[1]] = values.astype(BF16)
        copy = pltpu.make_async_copy(result.at[slot, :, pl.ds(0, values.shape[1])], target, out_sem.at[i])
        copy.start()
        stores.append(copy)

    loads[0].wait()
    loads[1].wait()
    for start in range(0, units, tile):
        at = pl.ds(start, tile)
        values = lax.dot_general(
            matrix(acts.at[0], at), matrix(grads, pl.ds(0, block)), ROWS_FIRST, preferred_element_type=F32
        )
        put(values, down_sum.at[at, :])
    for copy, copy_out in zip(moves, moves_out):
        copy.wait()
        copy_out.start()
    loads[2].wait()
    for kind, target in ((1, gate_sum), (2, up_sum)):
        loads[2 + kind].wait()
        for start in range(0, block, tile):
            at = pl.ds(start, tile)
            values = lax.dot_general(
                matrix(left, at), matrix(acts.at[kind], pl.ds(0, units)), ROWS_FIRST, preferred_element_type=F32
            )
            put(values, target.at[at, :])
    for copy in stores[-2:] + moves_out:
        copy.wait()


def per_device(tokens, expert_ids, gate_codes, w_gate, w_up, w_down, out_grad):
    experts = lax.axis_size("expert")
    groups = lax.axis_size("dp")
    lanes = experts // LINE
    tok_count, model_width = tokens.shape
    pair_count = tok_count * expert_ids.shape[1]
    capacity = 3 * pair_count // (2 * experts)
    capacity = -(-capacity // 16) * 16
    rows = experts * capacity
    half = lanes * capacity
    chunks = groups * max(1, PIECES // groups)
    ring = chunks // 2
    deep = half <= 96
    slots, lags = (2 * chunks, DEEP) if deep else (chunks, SHALLOW)
    width = model_width // chunks
    block = model_width // groups
    pieces = 2 * chunks
    gate_matrix, up_matrix, down_matrix = w_gate[0], w_up[0], w_down[0]
    units = gate_matrix.shape[1]
    vmem = pl.BlockSpec(memory_space=pltpu.VMEM)
    anywhere = pl.BlockSpec(memory_space=pl.ANY)
    dma = pltpu.SemaphoreType.DMA

    def shape(*dims):
        return jax.ShapeDtypeStruct(dims, BF16)

    def buffer(*dims):
        return pltpu.VMEM(dims, BF16)

    peers = max(1, lanes - 1)
    layer_out, tokens_grad, *factors = pl.pallas_call(
        functools.partial(exchange_kernel, lanes, capacity, groups, chunks, ring, slots, lags),
        out_shape=(
            shape(tok_count, model_width),
            shape(tok_count, model_width),
            shape(groups, rows, block),
            shape(groups, rows, block),
            shape(groups, rows, units),
            shape(groups, rows, units),
            shape(groups, rows, units),
        ),
        in_specs=[vmem] * 2 + [anywhere] * 5,
        out_specs=(anywhere,) * 7,
        scratch_shapes=[
            pltpu.VMEM((LINE, 2 * experts, tok_count), F32),
            buffer(LINE, chunks, tok_count, width),
            buffer(2, LINE, 2 * half, tok_count),
            buffer(2, LINE, tok_count, 2 * half),
            buffer(2, tok_count, half),
            buffer(chunks, lanes, LINE * capacity, width),
            buffer(chunks, lanes, 3 * capacity, width),
            buffer(pieces, rows, width),
            pltpu.VMEM((rows, units), F32),
            pltpu.VMEM((rows, units), F32),
            pltpu.VMEM((rows, units), F32),
            buffer(rows, units),
            buffer(rows, units),
            buffer(rows, units),
            buffer(chunks, units, width),
            buffer(ring, width, units),
            buffer(ring, width, units),
            buffer(chunks, lanes, LINE, capacity, width),
            buffer(slots, LINE, 2 * half, width),
            buffer(chunks, 2, tok_count, width),
            buffer(slots, 2, tok_count, width),
            buffer(chunks, tok_count, width),
            buffer(4, tok_count, width),
            dma((2,)),
            dma((LINE,)),
            dma((pieces,)),
            dma((pieces,)),
            dma((pieces, LINE)),
            dma((pieces,)),
            dma((pieces, peers)),
            dma((pieces, peers)),
            dma((pieces,)),
            dma((pieces,)),
            dma((pieces, peers)),
            dma((pieces, peers)),
            dma((pieces, 2)),
            dma((pieces, 2)),
            dma((pieces,)),
            dma((pieces,)),
            dma((pieces,)),
            dma((pieces,)),
            dma((pieces,)),
            dma((pieces, 2)),
            dma((chunks,)),
            dma((pieces,)),
            dma((pieces,)),
            dma((3, groups)),
            dma((3, groups)),
        ],
        compiler_params=pltpu.CompilerParams(
            collective_id=0, has_side_effects=True, vmem_limit_bytes=63 * MIB
        ),
    )(expert_ids.T, gate_codes.T, tokens, out_grad, gate_matrix, up_matrix, down_matrix)

    outs = pl.pallas_call(
        weights_kernel,
        out_shape=(
            shape(tok_count, model_width),
            shape(tok_count, model_width),
            shape(block, units),
            shape(block, units),
            shape(units, block),
        ),
        in_specs=[anywhere] * 7,
        out_specs=(anywhere,) * 5,
        scratch_shapes=[
            buffer(groups, rows, block),
            buffer(groups, rows, block),
            buffer(3, groups, rows, units),
            buffer(2, tok_count, model_width),
            buffer(2, 256, max(block, units)),
            dma((5,)),
            dma((4,)),
            dma((units // 256 + 2 * (block // 256),)),
        ],
        compiler_params=pltpu.CompilerParams(vmem_limit_bytes=56 * MIB),
    )(layer_out, tokens_grad, *factors)
    layer_out, tokens_grad, gate_sum, up_sum, down_sum = outs
    return layer_out, tokens_grad, gate_sum[None], up_sum[None], down_sum[None]


def solution(mesh):
    placed = (
        P(("dp", "expert"), None),
        P(("dp", "expert"), None),
        P(("dp", "expert"), None),
        P("expert", None, None),
        P("expert", None, None),
        P("expert", None, None),
        P(("dp", "expert"), None),
    )
    return jax.shard_map(
        per_device,
        mesh=mesh,
        in_specs=placed,
        out_specs=(
            P(("dp", "expert"), None),
            P(("dp", "expert"), None),
            P("expert", "dp", None),
            P("expert", "dp", None),
            P("expert", None, "dp"),
        ),
        check_vma=False,
    )
```

```python
import functools

import jax
import jax.numpy as jnp
from jax import lax
from jax.experimental import pallas as pl
from jax.experimental.pallas import tpu as pltpu
from jax.sharding import PartitionSpec as P

F32 = jnp.float32
BF16 = jnp.bfloat16
CONTRACT = (((1,), (1,)), ((), ()))
ROWS_FIRST = (((0,), (0,)), ((), ()))
LINE = 4
PIECES = 16
DEEP = (2, 1, 2, 4, 2, 4, 6, 8)
SHALLOW = (2, 1, 1, 2, 1, 2, 3, 3)
MIB = 2**20


def remote(src, dst, send, recv, peer):
    return pltpu.make_async_remote_copy(src_ref=src, dst_ref=dst, send_sem=send, recv_sem=recv, device_id=peer)


def exchange_kernel(
    lanes, cap, groups, chunks, ring, slots, lags,
    ids, codes, tokens, out_grad, w_gate, w_up, w_down,
    layer_out, tokens_grad, token_cols, grad_cols, all_hidden, all_gate, all_up,
    info, raw, sel, selt, half_selt, plane, mate_stage, landed, pre_gate, pre_up, hidden_grad,
    hidden, gate_pre, up_pre, vdown, vgate, vup, made, back, part_out, part_in, fin_out, out_stage,
    info_send, info_recv, raw_load, raw_send, raw_recv, forward_send, plane_send, plane_recv,
    mate_send, mate_recv, made_send, made_recv, back_send, back_recv, part_send, part_recv,
    fin_send, fin_recv, out_sem, weight_sem, down_sem, group_send, group_recv, act_send, act_recv,
):
    me = lax.axis_index("expert")
    group = lax.axis_index("dp")
    z = me // lanes
    y = me - z * lanes
    inner = (z + 1) // 2 == 1
    outer = (z + 1) // 2 != 1
    mate_z = z + 1 - 2 * lax.rem(z, 2)
    far_z = LINE - 1 - z
    mate = {"expert": mate_z * lanes + y}
    far = {"expert": far_z * lanes + y}
    onward = {"expert": jnp.where(inner, far_z, mate_z) * lanes + y}
    onward_slot = jnp.where(inner, 2, 1)
    experts = LINE * lanes
    tok_count, model_width = tokens.shape
    width = model_width // chunks
    block = model_width // groups
    per_block = chunks // groups
    pieces = 2 * chunks
    half = lanes * cap
    quad = LINE * cap
    sources = (tokens, out_grad)

    def lane_peer(j):
        return lax.rem(y + j, lanes)

    def group_peer(shift):
        return {"dp": lax.rem(group + shift, groups)}

    def mod(a, b):
        return a % b if isinstance(a, int) else lax.rem(a, b)

    def place(n):
        q = mod(n, chunks)
        order = q // per_block if isinstance(q, int) else lax.div(q, per_block)
        return mod(order + 1, groups), q - order * per_block

    def columns(n):
        shift, inside = place(n)
        start = lax.rem(group + shift, groups) * block + inside * width
        return pl.ds(pl.multiple_of(start, 128), width)

    def lane_rows(index, count):
        return pl.ds(pl.multiple_of(index * count, 16), count)

    def weight_loads(u):
        at, slot = columns(u), mod(u, ring)
        return (
            pltpu.make_async_copy(w_gate.at[at, :], vgate.at[slot], weight_sem.at[u, 0]),
            pltpu.make_async_copy(w_up.at[at, :], vup.at[slot], weight_sem.at[u, 1]),
        )

    def down_load(q):
        return pltpu.make_async_copy(w_down.at[:, columns(q)], vdown.at[q], down_sem.at[q])

    def load(n, kind):
        return pltpu.make_async_copy(sources[kind].at[:, columns(n)], raw.at[0, mod(n, chunks)], raw_load.at[n])

    def onwards(n, kind):
        return remote(
            sources[kind].at[:, columns(n)], raw.at[onward_slot, mod(n, chunks)],
            raw_send.at[n], raw_recv.at[n, onward_slot], onward,
        )

    def forwards(n):
        c = mod(n, chunks)
        return remote(raw.at[1, c], raw.at[3, c], forward_send.at[n], raw_recv.at[n, 3], far)

    def raw_from(n, s, peer):
        c = mod(n, chunks)
        return remote(raw.at[s, c], raw.at[s, c], raw_send.at[n], raw_recv.at[n, s], peer)

    def mates(n):
        c = mod(n, chunks)
        return remote(mate_stage.at[c], plane.at[c, :, pl.ds(cap, 3 * cap)], mate_send.at[n], mate_recv.at[n], mate)

    def planes(n):
        return [
            remote(
                plane.at[mod(n, chunks), lane_peer(j)], landed.at[n, lane_rows(y, quad)],
                plane_send.at[n, j - 1], plane_recv.at[n, j - 1], {"expert": z * lanes + lane_peer(j)},
            )
            for j in range(1, lanes)
        ]

    def mades(m):
        return [
            remote(
                made.at[mod(m, chunks), lane_peer(j)], back.at[mod(m, slots), :, lane_rows(y, cap)],
                made_send.at[m, j - 1], made_recv.at[m, j - 1], {"expert": z * lanes + lane_peer(j)},
            )
            for j in range(1, lanes)
        ]

    def backs(m):
        b = mod(m, slots)
        own_part, mate_part = pl.ds(0, half), pl.ds(half, half)
        return [
            remote(back.at[b, 1, own_part], back.at[b, 0, mate_part], back_send.at[m, 0], back_recv.at[m, 0], mate),
            remote(
                back.at[b, pl.ds(2, 2), own_part], back.at[b, pl.ds(2, 2), mate_part],
                back_send.at[m, 1], back_recv.at[m, 1], mate,
            ),
        ]

    def parts(m):
        return remote(part_out.at[mod(m, chunks)], part_in.at[mod(m, slots)], part_send.at[m], part_recv.at[m], far)

    def fins(m):
        return remote(fin_out.at[mod(m, chunks)], part_in.at[mod(m, slots), 0], fin_send.at[m], fin_recv.at[m], mate)

    def outs(m, kind):
        target = (layer_out, tokens_grad)[kind]
        return pltpu.make_async_copy(out_stage.at[mod(m, 4)], target.at[:, columns(m)], out_sem.at[m])

    info_onward = remote(info.at[0], info.at[onward_slot], info_send.at[0], info_recv.at[onward_slot], onward)
    info_forward = remote(info.at[1], info.at[3], info_send.at[1], info_recv.at[3], far)
    info_from_mate = remote(info.at[1], info.at[1], info_send.at[0], info_recv.at[1], mate)
    info_from_far = remote(info.at[2], info.at[2], info_send.at[0], info_recv.at[2], far)

    def to_group(source, target, shift, send, recv):
        if isinstance(shift, int) and shift == 0:
            return pltpu.make_async_copy(source, target, send)
        return remote(source, target, send, recv, group_peer(shift))

    def piece_to_group(n, kind, shift):
        at = pl.ds(pl.multiple_of(place(n)[1] * width, 128), width)
        slot = place(n)[0]
        target = (token_cols, grad_cols)[kind].at[slot, :, at]
        return to_group(landed.at[n], target, shift, group_send.at[n], group_recv.at[n])

    def act_to_group(kind, shift):
        source, target = ((hidden, all_hidden), (gate_pre, all_gate), (up_pre, all_up))[kind]
        return to_group(source, target.at[shift], shift, act_send.at[kind, shift], act_recv.at[kind, shift])

    def either(n, act):
        @pl.when(n < chunks)
        def _():
            act(0)

        @pl.when(n >= chunks)
        def _():
            act(1)

    lead = lags[0]
    for n in range(lead):
        load(n, 0).start()
    for u in range(ring):
        for copy in weight_loads(u):
            copy.start()
    barrier = pltpu.get_barrier_semaphore()
    for shift in range(1, groups):
        pl.semaphore_signal(barrier, inc=1, device_id=group_peer(shift))
    for j in range(1, lanes):
        pl.semaphore_signal(barrier, inc=1, device_id={"expert": z * lanes + lane_peer(j)})
    pl.semaphore_signal(barrier, inc=1, device_id=mate)

    @pl.when(inner)
    def _():
        pl.semaphore_signal(barrier, inc=1, device_id=far)
        pl.semaphore_wait(barrier, lanes + groups)

    @pl.when(outer)
    def _():
        pl.semaphore_wait(barrier, lanes + groups - 1)

    for n in range(lead):
        onwards(n, 0).start()

    expert_range = lax.broadcasted_iota(jnp.int32, (experts, tok_count), 0)
    named = [ids[k : k + 1, :] == expert_range for k in range(2)]
    chosen = jnp.where(named[0], 1.0, 0.0) + jnp.where(named[1], 1.0, 0.0)
    before = lax.broadcasted_iota(jnp.int32, (tok_count, tok_count), 0)
    after = lax.broadcasted_iota(jnp.int32, (tok_count, tok_count), 1)
    earlier = jnp.where(before < after, 1.0, 0.0).astype(BF16)
    ranks = jnp.dot(chosen.astype(BF16), earlier, preferred_element_type=F32)
    info[0, 0:experts] = jnp.where(chosen > 0.5, ranks, -1.0)
    gates = [jnp.where(named[k], codes[k : k + 1, :].astype(F32), 0.0) for k in range(2)]
    info[0, experts : 2 * experts] = (gates[0] + gates[1]) * (1.0 / 64.0)
    info_onward.start()
    for q in range(chunks):
        down_load(q).start()

    slot_range = lax.broadcasted_iota(jnp.int32, (cap, tok_count), 0).astype(F32)
    diagonal = jnp.where(before == after, 1.0, 0.0).astype(BF16)

    def select(s, planes_used):
        for p in range(planes_used):
            for lane in range(lanes):
                expert = (z, mate_z)[p] * lanes + lane
                hit = info[s, pl.ds(expert, 1), :] == slot_range
                gate = info[s, pl.ds(experts + expert, 1), :]
                at = pl.ds(p * half + lane * cap, cap)
                sel[0, s, at] = jnp.where(hit, 1.0, 0.0).astype(BF16)
                sel[1, s, at] = jnp.where(hit, gate, 0.0).astype(BF16)
        for kind in range(2):
            matrix = sel[kind, s, 0 : planes_used * half]
            turned = lax.dot_general(diagonal, matrix, CONTRACT, preferred_element_type=F32).astype(BF16)
            if planes_used == 2:
                selt[kind, s] = turned
            else:
                half_selt[kind] = turned

    @pl.when(inner)
    def _():
        select(0, 2)
        info_from_mate.wait_recv()
        info_forward.start()
        select(1, 1)
        info_from_far.wait_recv()
        select(2, 2)
        info_forward.wait_recv()
        select(3, 2)
        info_forward.wait_send()

    @pl.when(outer)
    def _():
        select(0, 1)

    info_onward.wait_send()

    for total in (pre_gate, pre_up, hidden_grad):
        total[...] = jnp.zeros_like(total)

    def spread(n, s, count):
        kind = lax.div(n, chunks)
        values = jnp.dot(sel[kind, s, 0:count], raw[s, mod(n, chunks)], preferred_element_type=F32)
        return values.astype(BF16)

    def into_plane(n, s, values):
        for lane in range(lanes):
            plane[mod(n, chunks), lane, s * cap : (s + 1) * cap] = values[lane * cap : (lane + 1) * cap]

    def keep_own(n):
        for copy in planes(n):
            copy.start()
        landed[n, lane_rows(y, quad)] = plane[mod(n, chunks), y]

    def stage_onward(n):
        @pl.when(n >= chunks)
        def _():
            for copy in planes(n - chunks):
                copy.wait_send()

        def act(kind):
            load(n, kind).start()
            onwards(n, kind).start()

        either(n, act)

    def stage_forward(n):
        @pl.when(inner)
        def _():
            raw_from(n, 1, mate).wait_recv()
            forwards(n).start()

    def stage_spread(n):
        c = mod(n, chunks)
        load(n, 0).wait()

        @pl.when(inner)
        def _():
            @pl.when(n >= 1)
            def _():
                forwards(n - 1).wait_send()

            @pl.when(n >= chunks)
            def _():
                mates(n - chunks).wait_send()

            def both(s, k):
                values = spread(n, s, 2 * half)
                into_plane(n, s, values[:half])
                for lane in range(lanes):
                    start = half + lane * cap
                    mate_stage[c, lane, k * cap : (k + 1) * cap] = values[start : start + cap]

            both(0, 0)
            into_plane(n, 1, spread(n, 1, half))
            raw_from(n, 2, far).wait_recv()
            both(2, 1)
            forwards(n).wait_recv()
            both(3, 2)
            mates(n).start()
            keep_own(n)

        @pl.when(outer)
        def _():
            into_plane(n, 0, spread(n, 0, half))

    def stage_relay(n):
        @pl.when(outer)
        def _():
            mates(n).wait_recv()
            keep_own(n)

    def stage_multiply(n):
        q = mod(n, chunks)
        for copy in planes(n):
            copy.wait_recv()
        shift = place(n)[0]

        def act(kind):
            @pl.when(shift == 0)
            def _():
                piece_to_group(n, kind, 0).start()

            if groups > 1:
                @pl.when(shift != 0)
                def _():
                    piece_to_group(n, kind, shift).start()

            rows = landed[n]
            if kind == 0:
                for copy in weight_loads(n):
                    copy.wait()
                for total, matrix in ((pre_gate, vgate), (pre_up, vup)):
                    total[...] += jnp.dot(rows, matrix[mod(n, ring)], preferred_element_type=F32)
                for copy in weight_loads(n + ring):
                    copy.start()
            else:
                hidden_grad[...] += lax.dot_general(rows, vdown[q], CONTRACT, preferred_element_type=F32)

        either(n, act)

        @pl.when(n == chunks - 1)
        def _():
            for p in range(chunks):
                down_load(p).wait()
            for start in range(0, pre_gate.shape[0], cap):
                at = pl.ds(start, cap)
                gate = pre_gate[at, :]
                hidden[at, :] = (gate * jax.nn.sigmoid(gate) * pre_up[at, :]).astype(BF16)
            send_act(0)

        @pl.when(n == pieces - 1)
        def _():
            for start in range(0, pre_gate.shape[0], cap):
                at = pl.ds(start, cap)
                gate, up, grad = pre_gate[at, :], pre_up[at, :], hidden_grad[at, :]
                sigmoid = jax.nn.sigmoid(gate)
                silu = gate * sigmoid
                gate_pre[at, :] = (grad * up * sigmoid * (1.0 + gate * (1.0 - sigmoid))).astype(BF16)
                up_pre[at, :] = (grad * silu).astype(BF16)
            send_act(1)
            send_act(2)

    def send_act(kind):
        for order in range(groups):
            act_to_group(kind, (order + 1) % groups).start()

    def stage_make(m):
        c = mod(m, chunks)

        def act(kind):
            if kind == 0:
                values = jnp.dot(hidden[...], vdown[c], preferred_element_type=F32)
            else:
                slot = mod(m, ring)
                for copy in weight_loads(m):
                    copy.wait()
                values = lax.dot_general(gate_pre[...], vgate[slot], CONTRACT, preferred_element_type=F32)
                values = values + lax.dot_general(up_pre[...], vup[slot], CONTRACT, preferred_element_type=F32)

                @pl.when(m + ring < pieces)
                def _():
                    for copy in weight_loads(m + ring):
                        copy.start()

                for copy in mades(m - chunks):
                    copy.wait_send()
            made[c] = values.astype(BF16).reshape(lanes, LINE, cap, width)

        either(m, act)
        for copy in mades(m):
            copy.start()
        back[mod(m, slots), :, lane_rows(y, cap)] = made[c, y]

    def stage_hand(m):
        @pl.when(outer)
        def _():
            for copy in mades(m):
                copy.wait_recv()
            for copy in backs(m):
                copy.start()

    def gather(m, s):
        kind = 1 - lax.div(m, chunks)
        return jnp.dot(selt[kind, s], back[mod(m, slots), s], preferred_element_type=F32)

    def gather_half(m, s):
        kind = 1 - lax.div(m, chunks)
        return jnp.dot(half_selt[kind], back[mod(m, slots), s, 0:half], preferred_element_type=F32)

    def stage_partial(m):
        c = mod(m, chunks)

        @pl.when(inner)
        def _():
            for copy in mades(m):
                copy.wait_recv()
            for copy in backs(m):
                copy.wait_recv()

            @pl.when(m >= chunks)
            def _():
                parts(m - chunks).wait_send()

            for s in (2, 3):
                part_out[c, s - 2] = gather(m, s).astype(BF16)
            parts(m).start()

    def put_out(m, values):
        @pl.when(m >= 4)
        def _():
            outs(m - 4, 0).wait()

        out_stage[mod(m, 4)] = values.astype(BF16)
        either(m, lambda kind: outs(m, kind).start())

    def stage_finish_inner(m):
        c, b = mod(m, chunks), mod(m, slots)

        @pl.when(inner)
        def _():
            @pl.when(m >= chunks)
            def _():
                fins(m - chunks).wait_send()

            near = gather_half(m, 1)
            own = gather(m, 0)
            parts(m).wait_recv()
            fin_out[c] = (near + part_in[b, 1].astype(F32)).astype(BF16)
            fins(m).start()
            put_out(m, own + part_in[b, 0].astype(F32))

    def stage_finish_outer(m):
        @pl.when(outer)
        def _():
            near = gather_half(m, 0)
            for copy in backs(m):
                copy.wait_send()
            fins(m).wait_recv()
            put_out(m, near + part_in[mod(m, slots), 0].astype(F32))

    _, ahead, relay, multiply, hand, partial, finish_inner, finish_outer = lags
    first_make = chunks + multiply
    stages = (
        (-lead, lead, stage_onward),
        (-ahead, ahead, stage_forward),
        (first_make + partial, 0, stage_partial),
        (0, 0, stage_spread),
        (first_make + hand, 0, stage_hand),
        (relay, 0, stage_relay),
        (first_make, 0, stage_make),
        (multiply, 0, stage_multiply),
        (first_make + finish_inner, 0, stage_finish_inner),
        (first_make + finish_outer, 0, stage_finish_outer),
    )
    for n in range(ahead):
        stage_forward(n)

    def run_tick(tick, carry):
        for lag, first, stage in stages:
            n = tick - lag

            @pl.when((n >= first) & (n < pieces))
            def _():
                stage(n)

        return carry

    lax.fori_loop(0, first_make + pieces + finish_outer, run_tick, 0)

    for n in range(pieces):
        onwards(n, n // chunks).wait_send()
    for n in range(chunks, pieces):
        for copy in planes(n):
            copy.wait_send()
    for m in range(chunks, pieces):
        for copy in mades(m):
            copy.wait_send()
    for m in range(pieces - 4, pieces):
        outs(m, 1).wait()

    @pl.when(inner)
    def _():
        forwards(pieces - 1).wait_send()
        for n in range(chunks, pieces):
            mates(n).wait_send()
        for m in range(chunks, pieces):
            parts(m).wait_send()
            fins(m).wait_send()

    group_copies = [(place(n)[0], piece_to_group(n, n // chunks, place(n)[0])) for n in range(pieces)]
    group_copies += [(shift, act_to_group(kind, shift)) for kind in range(3) for shift in range(groups)]
    for shift, copy in group_copies:
        if shift == 0:
            copy.wait()
        else:
            copy.wait_recv()
            copy.wait_send()


def weights_kernel(
    layer_in, tokens_in, token_cols, grad_cols, all_hidden, all_gate, all_up,
    layer_out, tokens_grad, gate_sum, up_sum, down_sum,
    left, grads, acts, moved, result, load_sem, move_sem, out_sem,
):
    through = ((layer_in, layer_out), (tokens_in, tokens_grad))
    moves = [pltpu.make_async_copy(a, moved.at[i], move_sem.at[i]) for i, (a, _) in enumerate(through)]
    moves_out = [pltpu.make_async_copy(moved.at[i], b, move_sem.at[2 + i]) for i, (_, b) in enumerate(through)]
    pairs = (
        (all_hidden, acts.at[0]), (grad_cols, grads), (token_cols, left), (all_gate, acts.at[1]), (all_up, acts.at[2])
    )
    loads = [pltpu.make_async_copy(a, b, load_sem.at[i]) for i, (a, b) in enumerate(pairs)]
    for copy in loads + moves:
        copy.start()
    depth = left.shape[0] * left.shape[1]
    block = left.shape[2]
    units = acts.shape[3]
    tile = 256
    stores = []

    def matrix(ref, at):
        return ref[:, :, at].reshape(depth, at.size)

    def put(values, target):
        i = len(stores)
        slot = i % 2
        if i >= 2:
            stores[i - 2].wait()
        result[slot, :, 0 : values.shape[1]] = values.astype(BF16)
        copy = pltpu.make_async_copy(result.at[slot, :, pl.ds(0, values.shape[1])], target, out_sem.at[i])
        copy.start()
        stores.append(copy)

    loads[0].wait()
    loads[1].wait()
    for start in range(0, units, tile):
        at = pl.ds(start, tile)
        values = lax.dot_general(
            matrix(acts.at[0], at), matrix(grads, pl.ds(0, block)), ROWS_FIRST, preferred_element_type=F32
        )
        put(values, down_sum.at[at, :])
    for copy, copy_out in zip(moves, moves_out):
        copy.wait()
        copy_out.start()
    loads[2].wait()
    for kind, target in ((1, gate_sum), (2, up_sum)):
        loads[2 + kind].wait()
        for start in range(0, block, tile):
            at = pl.ds(start, tile)
            values = lax.dot_general(
                matrix(left, at), matrix(acts.at[kind], pl.ds(0, units)), ROWS_FIRST, preferred_element_type=F32
            )
            put(values, target.at[at, :])
    for copy in stores[-2:] + moves_out:
        copy.wait()


def per_device(tokens, expert_ids, gate_codes, w_gate, w_up, w_down, out_grad):
    experts = lax.axis_size("expert")
    groups = lax.axis_size("dp")
    lanes = experts // LINE
    tok_count, model_width = tokens.shape
    pair_count = tok_count * expert_ids.shape[1]
    capacity = 3 * pair_count // (2 * experts)
    capacity = -(-capacity // 16) * 16
    rows = experts * capacity
    half = lanes * capacity
    chunks = groups * max(1, PIECES // groups)
    ring = chunks // 2
    deep = half <= 96
    slots, lags = (2 * chunks, DEEP) if deep else (chunks, SHALLOW)
    width = model_width // chunks
    block = model_width // groups
    pieces = 2 * chunks
    gate_matrix, up_matrix, down_matrix = w_gate[0], w_up[0], w_down[0]
    units = gate_matrix.shape[1]
    vmem = pl.BlockSpec(memory_space=pltpu.VMEM)
    anywhere = pl.BlockSpec(memory_space=pl.ANY)
    dma = pltpu.SemaphoreType.DMA

    def shape(*dims):
        return jax.ShapeDtypeStruct(dims, BF16)

    def buffer(*dims):
        return pltpu.VMEM(dims, BF16)

    peers = max(1, lanes - 1)
    layer_out, tokens_grad, *factors = pl.pallas_call(
        functools.partial(exchange_kernel, lanes, capacity, groups, chunks, ring, slots, lags),
        out_shape=(
            shape(tok_count, model_width),
            shape(tok_count, model_width),
            shape(groups, rows, block),
            shape(groups, rows, block),
            shape(groups, rows, units),
            shape(groups, rows, units),
            shape(groups, rows, units),
        ),
        in_specs=[vmem] * 2 + [anywhere] * 5,
        out_specs=(anywhere,) * 7,
        scratch_shapes=[
            pltpu.VMEM((LINE, 2 * experts, tok_count), F32),
            buffer(LINE, chunks, tok_count, width),
            buffer(2, LINE, 2 * half, tok_count),
            buffer(2, LINE, tok_count, 2 * half),
            buffer(2, tok_count, half),
            buffer(chunks, lanes, LINE * capacity, width),
            buffer(chunks, lanes, 3 * capacity, width),
            buffer(pieces, rows, width),
            pltpu.VMEM((rows, units), F32),
            pltpu.VMEM((rows, units), F32),
            pltpu.VMEM((rows, units), F32),
            buffer(rows, units),
            buffer(rows, units),
            buffer(rows, units),
            buffer(chunks, units, width),
            buffer(ring, width, units),
            buffer(ring, width, units),
            buffer(chunks, lanes, LINE, capacity, width),
            buffer(slots, LINE, 2 * half, width),
            buffer(chunks, 2, tok_count, width),
            buffer(slots, 2, tok_count, width),
            buffer(chunks, tok_count, width),
            buffer(4, tok_count, width),
            dma((2,)),
            dma((LINE,)),
            dma((pieces,)),
            dma((pieces,)),
            dma((pieces, LINE)),
            dma((pieces,)),
            dma((pieces, peers)),
            dma((pieces, peers)),
            dma((pieces,)),
            dma((pieces,)),
            dma((pieces, peers)),
            dma((pieces, peers)),
            dma((pieces, 2)),
            dma((pieces, 2)),
            dma((pieces,)),
            dma((pieces,)),
            dma((pieces,)),
            dma((pieces,)),
            dma((pieces,)),
            dma((pieces, 2)),
            dma((chunks,)),
            dma((pieces,)),
            dma((pieces,)),
            dma((3, groups)),
            dma((3, groups)),
        ],
        compiler_params=pltpu.CompilerParams(
            collective_id=0, has_side_effects=True, vmem_limit_bytes=63 * MIB
        ),
    )(expert_ids.T, gate_codes.T, tokens, out_grad, gate_matrix, up_matrix, down_matrix)

    outs = pl.pallas_call(
        weights_kernel,
        out_shape=(
            shape(tok_count, model_width),
            shape(tok_count, model_width),
            shape(block, units),
            shape(block, units),
            shape(units, block),
        ),
        in_specs=[anywhere] * 7,
        out_specs=(anywhere,) * 5,
        scratch_shapes=[
            buffer(groups, rows, block),
            buffer(groups, rows, block),
            buffer(3, groups, rows, units),
            buffer(2, tok_count, model_width),
            buffer(2, 256, max(block, units)),
            dma((5,)),
            dma((4,)),
            dma((units // 256 + 2 * (block // 256),)),
        ],
        compiler_params=pltpu.CompilerParams(vmem_limit_bytes=56 * MIB),
    )(layer_out, tokens_grad, *factors)
    layer_out, tokens_grad, gate_sum, up_sum, down_sum = outs
    return layer_out, tokens_grad, gate_sum[None], up_sum[None], down_sum[None]


def solution(mesh):
    placed = (
        P(("dp", "expert"), None),
        P(("dp", "expert"), None),
        P(("dp", "expert"), None),
        P("expert", None, None),
        P("expert", None, None),
        P("expert", None, None),
        P(("dp", "expert"), None),
    )
    return jax.shard_map(
        per_device,
        mesh=mesh,
        in_specs=placed,
        out_specs=(
            P(("dp", "expert"), None),
            P(("dp", "expert"), None),
            P("expert", "dp", None),
            P("expert", "dp", None),
            P("expert", None, "dp"),
        ),
        check_vma=False,
    )
```

```python
import functools

import jax
import jax.numpy as jnp
from jax import lax
from jax.experimental import pallas as pl
from jax.experimental.pallas import tpu as pltpu
from jax.sharding import PartitionSpec as P

F32 = jnp.float32
BF16 = jnp.bfloat16
CONTRACT = (((1,), (1,)), ((), ()))
ROWS_FIRST = (((0,), (0,)), ((), ()))
LINE = 4
MOVES = 1
PIECES = 16
DEEP = (2, 1, 2, 4, 2, 4, 6, 8)
SHALLOW = (2, 1, 1, 2, 1, 2, 3, 3)
SUMS = (8, 10, 14, 15)
MIB = 2**20


def remote(src, dst, send, recv, peer):
    return pltpu.make_async_remote_copy(src_ref=src, dst_ref=dst, send_sem=send, recv_sem=recv, device_id=peer)


def exchange_kernel(
    lanes, cap, groups, chunks, ring, slots, lags, sums,
    ids, codes, tokens, out_grad, w_gate, w_up, w_down,
    layer_out, tokens_grad, token_cols, grad_cols, all_hidden, all_gate, all_up, gate_sum, up_sum, down_sum,
    info, raw, sel, selt, half_selt, plane, mate_stage, landed, pre_gate, pre_up, hidden_grad,
    hidden, gate_pre, up_pre, vdown, vgate, vup, made, back, part_out, part_in, fin_out, out_stage, factors,
    info_send, info_recv, raw_load, raw_send, raw_recv, forward_send, plane_send, plane_recv,
    mate_send, mate_recv, made_send, made_recv, back_send, back_recv, part_send, part_recv,
    fin_send, fin_recv, out_sem, weight_sem, down_sem, group_send, group_recv, act_send, act_recv,
    swap_sem, factor_sem, sum_sem,
):
    me = lax.axis_index("expert")
    group = lax.axis_index("dp")
    z = me // lanes
    y = me - z * lanes
    inner = (z + 1) // 2 == 1
    outer = (z + 1) // 2 != 1
    mate_z = z + 1 - 2 * lax.rem(z, 2)
    far_z = LINE - 1 - z
    mate = {"expert": mate_z * lanes + y}
    far = {"expert": far_z * lanes + y}
    onward = {"expert": jnp.where(inner, far_z, mate_z) * lanes + y}
    onward_slot = jnp.where(inner, 2, 1)
    experts = LINE * lanes
    tok_count, model_width = tokens.shape
    width = model_width // chunks
    block = model_width // groups
    per_block = chunks // groups
    pieces = 2 * chunks
    half = lanes * cap
    quad = LINE * cap
    sources = (tokens, out_grad)

    def lane_peer(j):
        return lax.rem(y + j, lanes)

    def group_peer(shift):
        return {"dp": lax.rem(group + shift, groups)}

    def mod(a, b):
        return a % b if isinstance(a, int) else lax.rem(a, b)

    def place(n):
        q = mod(n, chunks)
        order = q // per_block if isinstance(q, int) else lax.div(q, per_block)
        return mod(order + 1, groups), q - order * per_block

    def columns(n):
        shift, inside = place(n)
        start = lax.rem(group + shift, groups) * block + inside * width
        return pl.ds(pl.multiple_of(start, 128), width)

    def lane_rows(index, count):
        return pl.ds(pl.multiple_of(index * count, 16), count)

    def weight_loads(u):
        at, slot = columns(u), mod(u, ring)
        return (
            pltpu.make_async_copy(w_gate.at[at, :], vgate.at[slot], weight_sem.at[u, 0]),
            pltpu.make_async_copy(w_up.at[at, :], vup.at[slot], weight_sem.at[u, 1]),
        )

    def down_load(q):
        return pltpu.make_async_copy(w_down.at[:, columns(q)], vdown.at[q], down_sem.at[q])

    def load(n, kind):
        return pltpu.make_async_copy(sources[kind].at[:, columns(n)], raw.at[0, mod(n, chunks)], raw_load.at[n])

    def onwards(n, kind):
        return remote(
            sources[kind].at[:, columns(n)], raw.at[onward_slot, mod(n, chunks)],
            raw_send.at[n], raw_recv.at[n, onward_slot], onward,
        )

    def forwards(n):
        c = mod(n, chunks)
        return remote(raw.at[1, c], raw.at[3, c], forward_send.at[n], raw_recv.at[n, 3], far)

    def raw_from(n, s, peer):
        c = mod(n, chunks)
        return remote(raw.at[s, c], raw.at[s, c], raw_send.at[n], raw_recv.at[n, s], peer)

    def mates(n):
        c = mod(n, chunks)
        return remote(mate_stage.at[c], plane.at[c, :, pl.ds(cap, 3 * cap)], mate_send.at[n], mate_recv.at[n], mate)

    def planes(n):
        return [
            remote(
                plane.at[mod(n, chunks), lane_peer(j)], landed.at[n, lane_rows(y, quad)],
                plane_send.at[n, j - 1], plane_recv.at[n, j - 1], {"expert": z * lanes + lane_peer(j)},
            )
            for j in range(1, lanes)
        ]

    def mades(m):
        return [
            remote(
                made.at[mod(m, chunks), lane_peer(j)], back.at[mod(m, slots), :, lane_rows(y, cap)],
                made_send.at[m, j - 1], made_recv.at[m, j - 1], {"expert": z * lanes + lane_peer(j)},
            )
            for j in range(1, lanes)
        ]

    def backs(m):
        b = mod(m, slots)
        own_part, mate_part = pl.ds(0, half), pl.ds(half, half)
        return [
            remote(back.at[b, 1, own_part], back.at[b, 0, mate_part], back_send.at[m, 0], back_recv.at[m, 0], mate),
            remote(
                back.at[b, pl.ds(2, 2), own_part], back.at[b, pl.ds(2, 2), mate_part],
                back_send.at[m, 1], back_recv.at[m, 1], mate,
            ),
        ]

    def parts(m):
        return remote(part_out.at[mod(m, chunks)], part_in.at[mod(m, slots)], part_send.at[m], part_recv.at[m], far)

    def fins(m):
        return remote(fin_out.at[mod(m, chunks)], part_in.at[mod(m, slots), 0], fin_send.at[m], fin_recv.at[m], mate)

    def outs(m, kind):
        target = (layer_out, tokens_grad)[kind]
        return pltpu.make_async_copy(out_stage.at[mod(m, 4)], target.at[:, columns(m)], out_sem.at[m])

    info_onward = remote(info.at[0], info.at[onward_slot], info_send.at[0], info_recv.at[onward_slot], onward)
    info_forward = remote(info.at[1], info.at[3], info_send.at[1], info_recv.at[3], far)
    info_from_mate = remote(info.at[1], info.at[1], info_send.at[0], info_recv.at[1], mate)
    info_from_far = remote(info.at[2], info.at[2], info_send.at[0], info_recv.at[2], far)

    def to_group(source, target, shift, send, recv):
        if isinstance(shift, int) and shift == 0:
            return pltpu.make_async_copy(source, target, send)
        return remote(source, target, send, recv, group_peer(shift))

    def piece_to_group(n, kind, shift):
        at = pl.ds(pl.multiple_of(place(n)[1] * width, 128), width)
        slot = place(n)[0]
        target = (token_cols, grad_cols)[kind].at[slot, :, at]
        return to_group(landed.at[n], target, shift, group_send.at[n], group_recv.at[n])

    def act_to_group(kind, shift):
        source, target = ((hidden, all_hidden), (gate_pre, all_gate), (up_pre, all_up))[kind]
        return to_group(source, target.at[shift], shift, act_send.at[kind, shift], act_recv.at[kind, shift])

    def either(n, act):
        @pl.when(n < chunks)
        def _():
            act(0)

        @pl.when(n >= chunks)
        def _():
            act(1)

    lead = lags[0]
    for n in range(lead):
        load(n, 0).start()
    for u in range(ring):
        for copy in weight_loads(u):
            copy.start()
    barrier = pltpu.get_barrier_semaphore()
    for shift in range(1, groups):
        pl.semaphore_signal(barrier, inc=1, device_id=group_peer(shift))
    for j in range(1, lanes):
        pl.semaphore_signal(barrier, inc=1, device_id={"expert": z * lanes + lane_peer(j)})
    pl.semaphore_signal(barrier, inc=1, device_id=mate)

    @pl.when(inner)
    def _():
        pl.semaphore_signal(barrier, inc=1, device_id=far)
        pl.semaphore_wait(barrier, lanes + groups)

    @pl.when(outer)
    def _():
        pl.semaphore_wait(barrier, lanes + groups - 1)

    for n in range(lead):
        onwards(n, 0).start()

    expert_range = lax.broadcasted_iota(jnp.int32, (experts, tok_count), 0)
    named = [ids[k : k + 1, :] == expert_range for k in range(2)]
    chosen = jnp.where(named[0], 1.0, 0.0) + jnp.where(named[1], 1.0, 0.0)
    before = lax.broadcasted_iota(jnp.int32, (tok_count, tok_count), 0)
    after = lax.broadcasted_iota(jnp.int32, (tok_count, tok_count), 1)
    earlier = jnp.where(before < after, 1.0, 0.0).astype(BF16)
    ranks = jnp.dot(chosen.astype(BF16), earlier, preferred_element_type=F32)
    info[0, 0:experts] = jnp.where(chosen > 0.5, ranks, -1.0)
    gates = [jnp.where(named[k], codes[k : k + 1, :].astype(F32), 0.0) for k in range(2)]
    info[0, experts : 2 * experts] = (gates[0] + gates[1]) * (1.0 / 64.0)
    info_onward.start()
    for q in range(chunks):
        down_load(q).start()

    slot_range = lax.broadcasted_iota(jnp.int32, (cap, tok_count), 0).astype(F32)
    diagonal = jnp.where(before == after, 1.0, 0.0).astype(BF16)

    def select(s, planes_used):
        for p in range(planes_used):
            for lane in range(lanes):
                expert = (z, mate_z)[p] * lanes + lane
                hit = info[s, pl.ds(expert, 1), :] == slot_range
                gate = info[s, pl.ds(experts + expert, 1), :]
                at = pl.ds(p * half + lane * cap, cap)
                sel[0, s, at] = jnp.where(hit, 1.0, 0.0).astype(BF16)
                sel[1, s, at] = jnp.where(hit, gate, 0.0).astype(BF16)
        for kind in range(2):
            matrix = sel[kind, s, 0 : planes_used * half]
            turned = lax.dot_general(diagonal, matrix, CONTRACT, preferred_element_type=F32).astype(BF16)
            if planes_used == 2:
                selt[kind, s] = turned
            else:
                half_selt[kind] = turned

    @pl.when(inner)
    def _():
        select(0, 2)
        info_from_mate.wait_recv()
        info_forward.start()
        select(1, 1)
        info_from_far.wait_recv()
        select(2, 2)
        info_forward.wait_recv()
        select(3, 2)
        info_forward.wait_send()

    @pl.when(outer)
    def _():
        select(0, 1)

    info_onward.wait_send()

    for total in (pre_gate, pre_up, hidden_grad):
        total[...] = jnp.zeros_like(total)

    def spread(n, s, count):
        kind = lax.div(n, chunks)
        values = jnp.dot(sel[kind, s, 0:count], raw[s, mod(n, chunks)], preferred_element_type=F32)
        return values.astype(BF16)

    def into_plane(n, s, values):
        for lane in range(lanes):
            plane[mod(n, chunks), lane, s * cap : (s + 1) * cap] = values[lane * cap : (lane + 1) * cap]

    def keep_own(n):
        for copy in planes(n):
            copy.start()
        landed[n, lane_rows(y, quad)] = plane[mod(n, chunks), y]

    def stage_onward(n):
        @pl.when(n >= chunks)
        def _():
            for copy in planes(n - chunks):
                copy.wait_send()

        def act(kind):
            load(n, kind).start()
            onwards(n, kind).start()

        either(n, act)

    def stage_forward(n):
        @pl.when(inner)
        def _():
            raw_from(n, 1, mate).wait_recv()
            forwards(n).start()

    def stage_spread(n):
        c = mod(n, chunks)
        load(n, 0).wait()

        @pl.when(inner)
        def _():
            @pl.when(n >= 1)
            def _():
                forwards(n - 1).wait_send()

            @pl.when(n >= chunks)
            def _():
                mates(n - chunks).wait_send()

            def both(s, k):
                values = spread(n, s, 2 * half)
                into_plane(n, s, values[:half])
                for lane in range(lanes):
                    start = half + lane * cap
                    mate_stage[c, lane, k * cap : (k + 1) * cap] = values[start : start + cap]

            both(0, 0)
            into_plane(n, 1, spread(n, 1, half))
            raw_from(n, 2, far).wait_recv()
            both(2, 1)
            forwards(n).wait_recv()
            both(3, 2)
            mates(n).start()
            keep_own(n)

        @pl.when(outer)
        def _():
            into_plane(n, 0, spread(n, 0, half))

    def stage_relay(n):
        @pl.when(outer)
        def _():
            mates(n).wait_recv()
            keep_own(n)

    def stage_multiply(n):
        q = mod(n, chunks)
        for copy in planes(n):
            copy.wait_recv()
        shift = place(n)[0]

        def act(kind):
            if not sums:
                @pl.when(shift == 0)
                def _():
                    piece_to_group(n, kind, 0).start()

            if groups > 1:
                @pl.when(shift != 0)
                def _():
                    piece_to_group(n, kind, shift).start()

            rows = landed[n]
            if kind == 0:
                for copy in weight_loads(n):
                    copy.wait()
                for total, matrix in ((pre_gate, vgate), (pre_up, vup)):
                    total[...] += jnp.dot(rows, matrix[mod(n, ring)], preferred_element_type=F32)
                for copy in weight_loads(n + ring):
                    copy.start()
            else:
                hidden_grad[...] += lax.dot_general(rows, vdown[q], CONTRACT, preferred_element_type=F32)

        either(n, act)

        @pl.when(n == chunks - 1)
        def _():
            for p in range(chunks):
                down_load(p).wait()
            for start in range(0, pre_gate.shape[0], cap):
                at = pl.ds(start, cap)
                gate = pre_gate[at, :]
                hidden[at, :] = (gate * jax.nn.sigmoid(gate) * pre_up[at, :]).astype(BF16)
            send_act(0)

        @pl.when(n == pieces - 1)
        def _():
            for start in range(0, pre_gate.shape[0], cap):
                at = pl.ds(start, cap)
                gate, up, grad = pre_gate[at, :], pre_up[at, :], hidden_grad[at, :]
                sigmoid = jax.nn.sigmoid(gate)
                silu = gate * sigmoid
                gate_pre[at, :] = (grad * up * sigmoid * (1.0 + gate * (1.0 - sigmoid))).astype(BF16)
                up_pre[at, :] = (grad * silu).astype(BF16)
            send_act(1)
            send_act(2)

    def send_act(kind):
        for shift in list(range(1, groups)) + ([] if sums else [0]):
            act_to_group(kind, shift).start()

    def stage_make(m):
        c = mod(m, chunks)

        def act(kind):
            if kind == 0:
                values = jnp.dot(hidden[...], vdown[c], preferred_element_type=F32)
            else:
                slot = mod(m, ring)
                for copy in weight_loads(m):
                    copy.wait()
                values = lax.dot_general(gate_pre[...], vgate[slot], CONTRACT, preferred_element_type=F32)
                values = values + lax.dot_general(up_pre[...], vup[slot], CONTRACT, preferred_element_type=F32)

                @pl.when(m + ring < pieces)
                def _():
                    for copy in weight_loads(m + ring):
                        copy.start()

                for copy in mades(m - chunks):
                    copy.wait_send()
            made[c] = values.astype(BF16).reshape(lanes, LINE, cap, width)

        either(m, act)
        for copy in mades(m):
            copy.start()
        back[mod(m, slots), :, lane_rows(y, cap)] = made[c, y]

    def stage_hand(m):
        @pl.when(outer)
        def _():
            for copy in mades(m):
                copy.wait_recv()
            for copy in backs(m):
                copy.start()

    def gather(m, s):
        kind = 1 - lax.div(m, chunks)
        return jnp.dot(selt[kind, s], back[mod(m, slots), s], preferred_element_type=F32)

    def gather_half(m, s):
        kind = 1 - lax.div(m, chunks)
        return jnp.dot(half_selt[kind], back[mod(m, slots), s, 0:half], preferred_element_type=F32)

    def stage_partial(m):
        c = mod(m, chunks)

        @pl.when(inner)
        def _():
            for copy in mades(m):
                copy.wait_recv()
            for copy in backs(m):
                copy.wait_recv()

            @pl.when(m >= chunks)
            def _():
                parts(m - chunks).wait_send()

            for s in (2, 3):
                part_out[c, s - 2] = gather(m, s).astype(BF16)
            parts(m).start()

    def put_out(m, values):
        @pl.when(m >= 4)
        def _():
            outs(m - 4, 0).wait()

        out_stage[mod(m, 4)] = values.astype(BF16)
        either(m, lambda kind: outs(m, kind).start())

    def stage_finish_inner(m):
        c, b = mod(m, chunks), mod(m, slots)

        @pl.when(inner)
        def _():
            @pl.when(m >= chunks)
            def _():
                fins(m - chunks).wait_send()

            near = gather_half(m, 1)
            own = gather(m, 0)
            parts(m).wait_recv()
            fin_out[c] = (near + part_in[b, 1].astype(F32)).astype(BF16)
            fins(m).start()
            put_out(m, own + part_in[b, 0].astype(F32))

    def stage_finish_outer(m):
        @pl.when(outer)
        def _():
            near = gather_half(m, 0)
            for copy in backs(m):
                copy.wait_send()
            fins(m).wait_recv()
            put_out(m, near + part_in[mod(m, slots), 0].astype(F32))

    def swap_load(n, kind):
        shift, inside = place(n)
        source = (token_cols, grad_cols)[kind].at[shift, :, pl.ds(inside * width, width)]
        return pltpu.make_async_copy(source, landed.at[n], swap_sem.at[n])

    def factor_load(kind, shift):
        source = (all_hidden, all_gate, all_up)[kind].at[shift]
        return pltpu.make_async_copy(source, factors.at[kind // 2, shift - 1], factor_sem.at[kind, shift])

    away = [(n, n // chunks) for n in range(pieces) if place(n)[0] != 0]

    def swap_acts(kind):
        for shift in range(1, groups):
            copy = act_to_group(kind, shift)
            copy.wait_send()
            copy.wait_recv()
            factor_load(kind, shift).start()

    def stage_swap(_):
        for n, kind in away:
            copy = piece_to_group(n, kind, place(n)[0])
            copy.wait_send()
            copy.wait_recv()
            swap_load(n, kind).start()
        swap_acts(0)

    def stage_swap_acts(_):
        swap_acts(1)
        swap_acts(2)

    def summed(kind, i):
        own = (hidden, gate_pre, up_pre)[kind]
        total = None
        for shift in range(groups):
            act = own[...] if shift == 0 else factors[kind // 2, shift - 1]
            piece = landed[(chunks if kind == 0 else 0) + (shift + groups - 1) % groups * per_block + i]
            pair = (act, piece) if kind == 0 else (piece, act)
            term = lax.dot_general(*pair, ROWS_FIRST, preferred_element_type=F32)
            total = term if total is None else total + term
        return total.astype(BF16)

    def sum_out(kind, i):
        at = pl.ds(pl.multiple_of(i * width, 128), width)
        held, target = ((vdown, down_sum.at[:, at]), (vgate, gate_sum.at[at, :]), (vup, up_sum.at[at, :]))[kind]
        return pltpu.make_async_copy(held.at[i], target, sum_sem.at[kind, i])

    def stage_sum_down(i):
        @pl.when(i == 0)
        def _():
            for n, kind in away:
                swap_load(n, kind).wait()
            for shift in range(1, groups):
                factor_load(0, shift).wait()

        vdown[i] = summed(0, i)
        sum_out(0, i).start()

    def stage_sum_gate_up(i):
        @pl.when(i == 0)
        def _():
            for kind in (1, 2):
                for shift in range(1, groups):
                    factor_load(kind, shift).wait()

        vgate[i] = summed(1, i)
        sum_out(1, i).start()
        vup[i] = summed(2, i)
        sum_out(2, i).start()

    _, ahead, relay, multiply, hand, partial, finish_inner, finish_outer = lags
    first_make = chunks + multiply
    stages = [
        (-lead, lead, stage_onward),
        (-ahead, ahead, stage_forward),
        (first_make + partial, 0, stage_partial),
        (0, 0, stage_spread),
        (first_make + hand, 0, stage_hand),
        (relay, 0, stage_relay),
        (first_make, 0, stage_make),
        (multiply, 0, stage_multiply),
        (first_make + finish_inner, 0, stage_finish_inner),
        (first_make + finish_outer, 0, stage_finish_outer),
    ]
    stages = [(lag, first, pieces, stage) for lag, first, stage in stages]
    ticks = first_make + pieces + finish_outer
    if sums:
        begin = first_make + chunks
        stages += [
            (begin + sums[0], 0, 1, stage_swap),
            (begin + sums[1], 0, per_block, stage_sum_down),
            (begin + sums[2], 0, 1, stage_swap_acts),
            (begin + sums[3], 0, per_block, stage_sum_gate_up),
        ]
        ticks = max(ticks, begin + sums[3] + per_block)
    for n in range(ahead):
        stage_forward(n)

    def run_tick(tick, carry):
        for lag, first, end, stage in stages:
            n = tick - lag

            @pl.when((n >= first) & (n < end))
            def _():
                stage(n)

        return carry

    lax.fori_loop(0, ticks, run_tick, 0)

    for n in range(pieces):
        onwards(n, n // chunks).wait_send()
    for n in range(chunks, pieces):
        for copy in planes(n):
            copy.wait_send()
    for m in range(chunks, pieces):
        for copy in mades(m):
            copy.wait_send()
    for m in range(pieces - 4, pieces):
        outs(m, 1).wait()

    @pl.when(inner)
    def _():
        forwards(pieces - 1).wait_send()
        for n in range(chunks, pieces):
            mates(n).wait_send()
        for m in range(chunks, pieces):
            parts(m).wait_send()
            fins(m).wait_send()

    if sums:
        for kind in range(3):
            for i in range(per_block):
                sum_out(kind, i).wait()
        return
    group_copies = [(place(n)[0], piece_to_group(n, n // chunks, place(n)[0])) for n in range(pieces)]
    group_copies += [(shift, act_to_group(kind, shift)) for kind in range(3) for shift in range(groups)]
    for shift, copy in group_copies:
        if shift == 0:
            copy.wait()
        else:
            copy.wait_recv()
            copy.wait_send()


def weights_kernel(
    layer_in, tokens_in, token_cols, grad_cols, all_hidden, all_gate, all_up,
    layer_out, tokens_grad, gate_sum, up_sum, down_sum,
    left, grads, acts, moved, result, load_sem, move_sem, out_sem,
):
    through = ((layer_in, layer_out), (tokens_in, tokens_grad))
    moves = [pltpu.make_async_copy(a, moved.at[i], move_sem.at[i]) for i, (a, _) in enumerate(through)]
    moves_out = [pltpu.make_async_copy(moved.at[i], b, move_sem.at[2 + i]) for i, (_, b) in enumerate(through)]
    pairs = (
        (all_hidden, acts.at[0]), (grad_cols, grads), (token_cols, left), (all_gate, acts.at[1]), (all_up, acts.at[2])
    )
    loads = [pltpu.make_async_copy(a, b, load_sem.at[i]) for i, (a, b) in enumerate(pairs)]
    for copy in loads + moves:
        copy.start()
    depth = left.shape[0] * left.shape[1]
    block = left.shape[2]
    units = acts.shape[3]
    tile = 256
    stores = []

    def matrix(ref, at):
        return ref[:, :, at].reshape(depth, at.size)

    def put(values, target):
        i = len(stores)
        slot = i % 2
        if i >= 2:
            stores[i - 2].wait()
        result[slot, :, 0 : values.shape[1]] = values.astype(BF16)
        copy = pltpu.make_async_copy(result.at[slot, :, pl.ds(0, values.shape[1])], target, out_sem.at[i])
        copy.start()
        stores.append(copy)

    loads[0].wait()
    loads[1].wait()
    for start in range(0, units, tile):
        at = pl.ds(start, tile)
        values = lax.dot_general(
            matrix(acts.at[0], at), matrix(grads, pl.ds(0, block)), ROWS_FIRST, preferred_element_type=F32
        )
        put(values, down_sum.at[at, :])
    for copy, copy_out in zip(moves, moves_out):
        copy.wait()
        copy_out.start()
    loads[2].wait()
    for kind, target in ((1, gate_sum), (2, up_sum)):
        loads[2 + kind].wait()
        for start in range(0, block, tile):
            at = pl.ds(start, tile)
            values = lax.dot_general(
                matrix(left, at), matrix(acts.at[kind], pl.ds(0, units)), ROWS_FIRST, preferred_element_type=F32
            )
            put(values, target.at[at, :])
    for copy in stores[-2:] + moves_out:
        copy.wait()


def move_kernel(*refs):
    sources, targets, held, (in_sem, out_sem) = refs[:5], refs[5:10], refs[10:15], refs[15:]
    ins, outs = [], []
    for part in range(MOVES):
        for i in range(5):
            size = sources[i].shape[0] // MOVES
            at = pl.ds(part * size, size)
            ins.append(pltpu.make_async_copy(sources[i].at[at], held[i].at[at], in_sem.at[i, part]))
            outs.append(pltpu.make_async_copy(held[i].at[at], targets[i].at[at], out_sem.at[i, part]))
    for copy in ins:
        copy.start()
    for copy, copy_out in zip(ins, outs):
        copy.wait()
        copy_out.start()
    for copy in outs:
        copy.wait()


def per_device(tokens, expert_ids, gate_codes, w_gate, w_up, w_down, out_grad):
    experts = lax.axis_size("expert")
    groups = lax.axis_size("dp")
    lanes = experts // LINE
    tok_count, model_width = tokens.shape
    pair_count = tok_count * expert_ids.shape[1]
    capacity = 3 * pair_count // (2 * experts)
    capacity = -(-capacity // 16) * 16
    rows = experts * capacity
    half = lanes * capacity
    chunks = groups * max(1, PIECES // groups)
    ring = chunks // 2
    deep = half <= 96
    slots, lags, sums = (2 * chunks, DEEP, SUMS) if deep else (chunks, SHALLOW, None)
    width = model_width // chunks
    block = model_width // groups
    pieces = 2 * chunks
    gate_matrix, up_matrix, down_matrix = w_gate[0], w_up[0], w_down[0]
    units = gate_matrix.shape[1]
    vmem = pl.BlockSpec(memory_space=pltpu.VMEM)
    anywhere = pl.BlockSpec(memory_space=pl.ANY)
    dma = pltpu.SemaphoreType.DMA

    def shape(*dims):
        return jax.ShapeDtypeStruct(dims, BF16)

    def buffer(*dims):
        return pltpu.VMEM(dims, BF16)

    peers = max(1, lanes - 1)
    layer_out, tokens_grad, *others = pl.pallas_call(
        functools.partial(exchange_kernel, lanes, capacity, groups, chunks, ring, slots, lags, sums),
        out_shape=(
            shape(tok_count, model_width),
            shape(tok_count, model_width),
            shape(groups, rows, block),
            shape(groups, rows, block),
            shape(groups, rows, units),
            shape(groups, rows, units),
            shape(groups, rows, units),
            shape(block, units),
            shape(block, units),
            shape(units, block),
        ),
        in_specs=[vmem] * 2 + [anywhere] * 5,
        out_specs=(anywhere,) * 10,
        scratch_shapes=[
            pltpu.VMEM((LINE, 2 * experts, tok_count), F32),
            buffer(LINE, chunks, tok_count, width),
            buffer(2, LINE, 2 * half, tok_count),
            buffer(2, LINE, tok_count, 2 * half),
            buffer(2, tok_count, half),
            buffer(chunks, lanes, LINE * capacity, width),
            buffer(chunks, lanes, 3 * capacity, width),
            buffer(pieces, rows, width),
            pltpu.VMEM((rows, units), F32),
            pltpu.VMEM((rows, units), F32),
            pltpu.VMEM((rows, units), F32),
            buffer(rows, units),
            buffer(rows, units),
            buffer(rows, units),
            buffer(chunks, units, width),
            buffer(ring, width, units),
            buffer(ring, width, units),
            buffer(chunks, lanes, LINE, capacity, width),
            buffer(slots, LINE, 2 * half, width),
            buffer(chunks, 2, tok_count, width),
            buffer(slots, 2, tok_count, width),
            buffer(chunks, tok_count, width),
            buffer(4, tok_count, width),
            buffer(2, groups - 1, rows, units) if sums else buffer(16, 128),
            dma((2,)),
            dma((LINE,)),
            dma((pieces,)),
            dma((pieces,)),
            dma((pieces, LINE)),
            dma((pieces,)),
            dma((pieces, peers)),
            dma((pieces, peers)),
            dma((pieces,)),
            dma((pieces,)),
            dma((pieces, peers)),
            dma((pieces, peers)),
            dma((pieces, 2)),
            dma((pieces, 2)),
            dma((pieces,)),
            dma((pieces,)),
            dma((pieces,)),
            dma((pieces,)),
            dma((pieces,)),
            dma((pieces, 2)),
            dma((chunks,)),
            dma((pieces,)),
            dma((pieces,)),
            dma((3, groups)),
            dma((3, groups)),
            dma((pieces,)),
            dma((3, groups)),
            dma((3, chunks // groups)),
        ],
        compiler_params=pltpu.CompilerParams(
            collective_id=0, has_side_effects=True, vmem_limit_bytes=63 * MIB
        ),
    )(expert_ids.T, gate_codes.T, tokens, out_grad, gate_matrix, up_matrix, down_matrix)

    if sums:
        results = [layer_out, tokens_grad, *others[5:]]
        layer_out, tokens_grad, gate_sum, up_sum, down_sum = pl.pallas_call(
            move_kernel,
            out_shape=tuple(shape(*result.shape) for result in results),
            in_specs=[anywhere] * 5,
            out_specs=(anywhere,) * 5,
            scratch_shapes=[buffer(*result.shape) for result in results] + [dma((5, MOVES)), dma((5, MOVES))],
            compiler_params=pltpu.CompilerParams(vmem_limit_bytes=60 * MIB),
        )(*results)
        return layer_out, tokens_grad, gate_sum[None], up_sum[None], down_sum[None]

    outs = pl.pallas_call(
        weights_kernel,
        out_shape=(
            shape(tok_count, model_width),
            shape(tok_count, model_width),
            shape(block, units),
            shape(block, units),
            shape(units, block),
        ),
        in_specs=[anywhere] * 7,
        out_specs=(anywhere,) * 5,
        scratch_shapes=[
            buffer(groups, rows, block),
            buffer(groups, rows, block),
            buffer(3, groups, rows, units),
            buffer(2, tok_count, model_width),
            buffer(2, 256, max(block, units)),
            dma((5,)),
            dma((4,)),
            dma((units // 256 + 2 * (block // 256),)),
        ],
        compiler_params=pltpu.CompilerParams(vmem_limit_bytes=56 * MIB),
    )(layer_out, tokens_grad, *others[:5])
    layer_out, tokens_grad, gate_sum, up_sum, down_sum = outs
    return layer_out, tokens_grad, gate_sum[None], up_sum[None], down_sum[None]


def solution(mesh):
    placed = (
        P(("dp", "expert"), None),
        P(("dp", "expert"), None),
        P(("dp", "expert"), None),
        P("expert", None, None),
        P("expert", None, None),
        P("expert", None, None),
        P(("dp", "expert"), None),
    )
    return jax.shard_map(
        per_device,
        mesh=mesh,
        in_specs=placed,
        out_specs=(
            P(("dp", "expert"), None),
            P(("dp", "expert"), None),
            P("expert", "dp", None),
            P("expert", "dp", None),
            P("expert", None, "dp"),
        ),
        check_vma=False,
    )
```

```python
import functools

import jax
import jax.numpy as jnp
from jax import lax
from jax.experimental import pallas as pl
from jax.experimental.pallas import tpu as pltpu
from jax.sharding import PartitionSpec as P

F32 = jnp.float32
BF16 = jnp.bfloat16
CONTRACT = (((1,), (1,)), ((), ()))
ROWS_FIRST = (((0,), (0,)), ((), ()))
LINE = 4
MOVES = 1
PIECES = 16
DEEP = (2, 1, 2, 3, 2, 4, 6, 8)
SHALLOW = (2, 1, 1, 2, 1, 2, 3, 3)
SUMS = (8, 10, 15, 16)
MIB = 2**20


def remote(src, dst, send, recv, peer):
    return pltpu.make_async_remote_copy(src_ref=src, dst_ref=dst, send_sem=send, recv_sem=recv, device_id=peer)


def exchange_kernel(
    lanes, cap, groups, chunks, ring, slots, lags, sums,
    ids, codes, tokens, out_grad, w_gate, w_up, w_down,
    layer_out, tokens_grad, token_cols, grad_cols, all_hidden, all_gate, all_up, gate_sum, up_sum, down_sum,
    info, raw, sel, selt, half_selt, plane, mate_stage, landed, pre_gate, pre_up, hidden_grad,
    hidden, gate_pre, up_pre, vdown, vgate, vup, made, back, part_out, part_in, fin_out, out_stage, factors,
    info_send, info_recv, raw_load, raw_send, raw_recv, forward_send, plane_send, plane_recv,
    mate_send, mate_recv, made_send, made_recv, back_send, back_recv, part_send, part_recv,
    fin_send, fin_recv, out_sem, weight_sem, down_sem, group_send, group_recv, act_send, act_recv,
    swap_sem, factor_sem, sum_sem,
):
    me = lax.axis_index("expert")
    group = lax.axis_index("dp")
    z = me // lanes
    y = me - z * lanes
    inner = (z + 1) // 2 == 1
    outer = (z + 1) // 2 != 1
    mate_z = z + 1 - 2 * lax.rem(z, 2)
    far_z = LINE - 1 - z
    mate = {"expert": mate_z * lanes + y}
    far = {"expert": far_z * lanes + y}
    onward = {"expert": jnp.where(inner, far_z, mate_z) * lanes + y}
    onward_slot = jnp.where(inner, 2, 1)
    experts = LINE * lanes
    tok_count, model_width = tokens.shape
    width = model_width // chunks
    block = model_width // groups
    per_block = chunks // groups
    pieces = 2 * chunks
    half = lanes * cap
    quad = LINE * cap
    sources = (tokens, out_grad)

    def lane_peer(j):
        return lax.rem(y + j, lanes)

    def group_peer(shift):
        return {"dp": lax.rem(group + shift, groups)}

    def mod(a, b):
        return a % b if isinstance(a, int) else lax.rem(a, b)

    def place(n):
        q = mod(n, chunks)
        order = q // per_block if isinstance(q, int) else lax.div(q, per_block)
        return mod(order + 1, groups), q - order * per_block

    def columns(n):
        shift, inside = place(n)
        start = lax.rem(group + shift, groups) * block + inside * width
        return pl.ds(pl.multiple_of(start, 128), width)

    def lane_rows(index, count):
        return pl.ds(pl.multiple_of(index * count, 16), count)

    def weight_loads(u):
        at, slot = columns(u), mod(u, ring)
        return (
            pltpu.make_async_copy(w_gate.at[at, :], vgate.at[slot], weight_sem.at[u, 0]),
            pltpu.make_async_copy(w_up.at[at, :], vup.at[slot], weight_sem.at[u, 1]),
        )

    def down_load(q):
        return pltpu.make_async_copy(w_down.at[:, columns(q)], vdown.at[q], down_sem.at[q])

    def load(n, kind):
        return pltpu.make_async_copy(sources[kind].at[:, columns(n)], raw.at[0, mod(n, chunks)], raw_load.at[n])

    def onwards(n, kind):
        return remote(
            sources[kind].at[:, columns(n)], raw.at[onward_slot, mod(n, chunks)],
            raw_send.at[n], raw_recv.at[n, onward_slot], onward,
        )

    def forwards(n):
        c = mod(n, chunks)
        return remote(raw.at[1, c], raw.at[3, c], forward_send.at[n], raw_recv.at[n, 3], far)

    def raw_from(n, s, peer):
        c = mod(n, chunks)
        return remote(raw.at[s, c], raw.at[s, c], raw_send.at[n], raw_recv.at[n, s], peer)

    def mates(n):
        c = mod(n, chunks)
        return remote(mate_stage.at[c], plane.at[c, :, pl.ds(cap, 3 * cap)], mate_send.at[n], mate_recv.at[n], mate)

    def planes(n):
        return [
            remote(
                plane.at[mod(n, chunks), lane_peer(j)], landed.at[n, lane_rows(y, quad)],
                plane_send.at[n, j - 1], plane_recv.at[n, j - 1], {"expert": z * lanes + lane_peer(j)},
            )
            for j in range(1, lanes)
        ]

    def mades(m):
        return [
            remote(
                made.at[mod(m, chunks), lane_peer(j)], back.at[mod(m, slots), :, lane_rows(y, cap)],
                made_send.at[m, j - 1], made_recv.at[m, j - 1], {"expert": z * lanes + lane_peer(j)},
            )
            for j in range(1, lanes)
        ]

    def backs(m):
        b = mod(m, slots)
        own_part, mate_part = pl.ds(0, half), pl.ds(half, half)
        return [
            remote(back.at[b, 1, own_part], back.at[b, 0, mate_part], back_send.at[m, 0], back_recv.at[m, 0], mate),
            remote(
                back.at[b, pl.ds(2, 2), own_part], back.at[b, pl.ds(2, 2), mate_part],
                back_send.at[m, 1], back_recv.at[m, 1], mate,
            ),
        ]

    def parts(m):
        return remote(part_out.at[mod(m, chunks)], part_in.at[mod(m, slots)], part_send.at[m], part_recv.at[m], far)

    def fins(m):
        return remote(fin_out.at[mod(m, chunks)], part_in.at[mod(m, slots), 0], fin_send.at[m], fin_recv.at[m], mate)

    def outs(m, kind):
        target = (layer_out, tokens_grad)[kind]
        return pltpu.make_async_copy(out_stage.at[mod(m, 4)], target.at[:, columns(m)], out_sem.at[m])

    info_onward = remote(info.at[0], info.at[onward_slot], info_send.at[0], info_recv.at[onward_slot], onward)
    info_forward = remote(info.at[1], info.at[3], info_send.at[1], info_recv.at[3], far)
    info_from_mate = remote(info.at[1], info.at[1], info_send.at[0], info_recv.at[1], mate)
    info_from_far = remote(info.at[2], info.at[2], info_send.at[0], info_recv.at[2], far)

    def to_group(source, target, shift, send, recv):
        if isinstance(shift, int) and shift == 0:
            return pltpu.make_async_copy(source, target, send)
        return remote(source, target, send, recv, group_peer(shift))

    def piece_to_group(n, kind, shift):
        at = pl.ds(pl.multiple_of(place(n)[1] * width, 128), width)
        slot = place(n)[0]
        target = (token_cols, grad_cols)[kind].at[slot, :, at]
        return to_group(landed.at[n], target, shift, group_send.at[n], group_recv.at[n])

    def act_to_group(kind, shift):
        source, target = ((hidden, all_hidden), (gate_pre, all_gate), (up_pre, all_up))[kind]
        return to_group(source, target.at[shift], shift, act_send.at[kind, shift], act_recv.at[kind, shift])

    def either(n, act):
        @pl.when(n < chunks)
        def _():
            act(0)

        @pl.when(n >= chunks)
        def _():
            act(1)

    lead = lags[0]
    for n in range(lead):
        load(n, 0).start()
    for u in range(ring):
        for copy in weight_loads(u):
            copy.start()
    barrier = pltpu.get_barrier_semaphore()
    for shift in range(1, groups):
        pl.semaphore_signal(barrier, inc=1, device_id=group_peer(shift))
    for j in range(1, lanes):
        pl.semaphore_signal(barrier, inc=1, device_id={"expert": z * lanes + lane_peer(j)})
    pl.semaphore_signal(barrier, inc=1, device_id=mate)

    @pl.when(inner)
    def _():
        pl.semaphore_signal(barrier, inc=1, device_id=far)
        pl.semaphore_wait(barrier, lanes + groups)

    @pl.when(outer)
    def _():
        pl.semaphore_wait(barrier, lanes + groups - 1)

    for n in range(lead):
        onwards(n, 0).start()

    expert_range = lax.broadcasted_iota(jnp.int32, (experts, tok_count), 0)
    named = [ids[k : k + 1, :] == expert_range for k in range(2)]
    chosen = jnp.where(named[0], 1.0, 0.0) + jnp.where(named[1], 1.0, 0.0)
    before = lax.broadcasted_iota(jnp.int32, (tok_count, tok_count), 0)
    after = lax.broadcasted_iota(jnp.int32, (tok_count, tok_count), 1)
    earlier = jnp.where(before < after, 1.0, 0.0).astype(BF16)
    ranks = jnp.dot(chosen.astype(BF16), earlier, preferred_element_type=F32)
    info[0, 0:experts] = jnp.where(chosen > 0.5, ranks, -1.0)
    gates = [jnp.where(named[k], codes[k : k + 1, :].astype(F32), 0.0) for k in range(2)]
    info[0, experts : 2 * experts] = (gates[0] + gates[1]) * (1.0 / 64.0)
    info_onward.start()
    for q in range(chunks):
        down_load(q).start()

    slot_range = lax.broadcasted_iota(jnp.int32, (cap, tok_count), 0).astype(F32)
    diagonal = jnp.where(before == after, 1.0, 0.0).astype(BF16)

    def select(s, planes_used):
        for p in range(planes_used):
            for lane in range(lanes):
                expert = (z, mate_z)[p] * lanes + lane
                hit = info[s, pl.ds(expert, 1), :] == slot_range
                gate = info[s, pl.ds(experts + expert, 1), :]
                at = pl.ds(p * half + lane * cap, cap)
                sel[0, s, at] = jnp.where(hit, 1.0, 0.0).astype(BF16)
                sel[1, s, at] = jnp.where(hit, gate, 0.0).astype(BF16)
        for kind in range(2):
            matrix = sel[kind, s, 0 : planes_used * half]
            turned = lax.dot_general(diagonal, matrix, CONTRACT, preferred_element_type=F32).astype(BF16)
            if planes_used == 2:
                selt[kind, s] = turned
            else:
                half_selt[kind] = turned

    @pl.when(inner)
    def _():
        select(0, 2)
        info_from_mate.wait_recv()
        info_forward.start()
        select(1, 1)
        info_from_far.wait_recv()
        select(2, 2)
        info_forward.wait_recv()
        select(3, 2)
        info_forward.wait_send()

    @pl.when(outer)
    def _():
        select(0, 1)

    info_onward.wait_send()

    for total in (pre_gate, pre_up, hidden_grad):
        total[...] = jnp.zeros_like(total)

    def spread(n, s, count):
        kind = lax.div(n, chunks)
        values = jnp.dot(sel[kind, s, 0:count], raw[s, mod(n, chunks)], preferred_element_type=F32)
        return values.astype(BF16)

    def into_plane(n, s, values):
        for lane in range(lanes):
            plane[mod(n, chunks), lane, s * cap : (s + 1) * cap] = values[lane * cap : (lane + 1) * cap]

    def keep_own(n):
        for copy in planes(n):
            copy.start()
        landed[n, lane_rows(y, quad)] = plane[mod(n, chunks), y]

    def stage_onward(n):
        @pl.when(n >= chunks)
        def _():
            for copy in planes(n - chunks):
                copy.wait_send()

        def act(kind):
            load(n, kind).start()
            onwards(n, kind).start()

        either(n, act)

    def stage_forward(n):
        @pl.when(inner)
        def _():
            raw_from(n, 1, mate).wait_recv()
            forwards(n).start()

    def stage_spread(n):
        c = mod(n, chunks)
        load(n, 0).wait()

        @pl.when(inner)
        def _():
            @pl.when(n >= 1)
            def _():
                forwards(n - 1).wait_send()

            @pl.when(n >= chunks)
            def _():
                mates(n - chunks).wait_send()

            def both(s, k):
                values = spread(n, s, 2 * half)
                into_plane(n, s, values[:half])
                for lane in range(lanes):
                    start = half + lane * cap
                    mate_stage[c, lane, k * cap : (k + 1) * cap] = values[start : start + cap]

            both(0, 0)
            into_plane(n, 1, spread(n, 1, half))
            raw_from(n, 2, far).wait_recv()
            both(2, 1)
            forwards(n).wait_recv()
            both(3, 2)
            mates(n).start()
            keep_own(n)

        @pl.when(outer)
        def _():
            into_plane(n, 0, spread(n, 0, half))

    def stage_relay(n):
        @pl.when(outer)
        def _():
            mates(n).wait_recv()
            keep_own(n)

    def stage_multiply(n):
        q = mod(n, chunks)
        for copy in planes(n):
            copy.wait_recv()
        shift = place(n)[0]

        def act(kind):
            if not sums:
                @pl.when(shift == 0)
                def _():
                    piece_to_group(n, kind, 0).start()

            if groups > 1:
                @pl.when(shift != 0)
                def _():
                    piece_to_group(n, kind, shift).start()

            rows = landed[n]
            if kind == 0:
                for copy in weight_loads(n):
                    copy.wait()
                for total, matrix in ((pre_gate, vgate), (pre_up, vup)):
                    total[...] += jnp.dot(rows, matrix[mod(n, ring)], preferred_element_type=F32)
                for copy in weight_loads(n + ring):
                    copy.start()
            else:
                hidden_grad[...] += lax.dot_general(rows, vdown[q], CONTRACT, preferred_element_type=F32)

        either(n, act)

        @pl.when(n == chunks - 1)
        def _():
            for p in range(chunks):
                down_load(p).wait()
            for start in range(0, pre_gate.shape[0], cap):
                at = pl.ds(start, cap)
                gate = pre_gate[at, :]
                hidden[at, :] = (gate * jax.nn.sigmoid(gate) * pre_up[at, :]).astype(BF16)
            send_act(0)

        @pl.when(n == pieces - 1)
        def _():
            for start in range(0, pre_gate.shape[0], cap):
                at = pl.ds(start, cap)
                gate, up, grad = pre_gate[at, :], pre_up[at, :], hidden_grad[at, :]
                sigmoid = jax.nn.sigmoid(gate)
                silu = gate * sigmoid
                gate_pre[at, :] = (grad * up * sigmoid * (1.0 + gate * (1.0 - sigmoid))).astype(BF16)
                up_pre[at, :] = (grad * silu).astype(BF16)
            send_act(1)
            send_act(2)

    def send_act(kind):
        for shift in list(range(1, groups)) + ([] if sums else [0]):
            act_to_group(kind, shift).start()

    def stage_make(m):
        c = mod(m, chunks)

        def act(kind):
            if kind == 0:
                values = jnp.dot(hidden[...], vdown[c], preferred_element_type=F32)
            else:
                slot = mod(m, ring)
                for copy in weight_loads(m):
                    copy.wait()
                values = lax.dot_general(gate_pre[...], vgate[slot], CONTRACT, preferred_element_type=F32)
                values = values + lax.dot_general(up_pre[...], vup[slot], CONTRACT, preferred_element_type=F32)

                @pl.when(m + ring < pieces)
                def _():
                    for copy in weight_loads(m + ring):
                        copy.start()

                for copy in mades(m - chunks):
                    copy.wait_send()
            made[c] = values.astype(BF16).reshape(lanes, LINE, cap, width)

        either(m, act)
        for copy in mades(m):
            copy.start()
        back[mod(m, slots), :, lane_rows(y, cap)] = made[c, y]

    def stage_hand(m):
        @pl.when(outer)
        def _():
            for copy in mades(m):
                copy.wait_recv()
            for copy in backs(m):
                copy.start()

    def gather(m, s):
        kind = 1 - lax.div(m, chunks)
        return jnp.dot(selt[kind, s], back[mod(m, slots), s], preferred_element_type=F32)

    def gather_half(m, s):
        kind = 1 - lax.div(m, chunks)
        return jnp.dot(half_selt[kind], back[mod(m, slots), s, 0:half], preferred_element_type=F32)

    def stage_partial(m):
        c = mod(m, chunks)

        @pl.when(inner)
        def _():
            for copy in mades(m):
                copy.wait_recv()
            for copy in backs(m):
                copy.wait_recv()

            @pl.when(m >= chunks)
            def _():
                parts(m - chunks).wait_send()

            for s in (2, 3):
                part_out[c, s - 2] = gather(m, s).astype(BF16)
            parts(m).start()

    def put_out(m, values):
        @pl.when(m >= 4)
        def _():
            outs(m - 4, 0).wait()

        out_stage[mod(m, 4)] = values.astype(BF16)
        either(m, lambda kind: outs(m, kind).start())

    def stage_finish_inner(m):
        c, b = mod(m, chunks), mod(m, slots)

        @pl.when(inner)
        def _():
            @pl.when(m >= chunks)
            def _():
                fins(m - chunks).wait_send()

            near = gather_half(m, 1)
            own = gather(m, 0)
            parts(m).wait_recv()
            fin_out[c] = (near + part_in[b, 1].astype(F32)).astype(BF16)
            fins(m).start()
            put_out(m, own + part_in[b, 0].astype(F32))

    def stage_finish_outer(m):
        @pl.when(outer)
        def _():
            near = gather_half(m, 0)
            for copy in backs(m):
                copy.wait_send()
            fins(m).wait_recv()
            put_out(m, near + part_in[mod(m, slots), 0].astype(F32))

    def swap_load(n, kind):
        shift, inside = place(n)
        source = (token_cols, grad_cols)[kind].at[shift, :, pl.ds(inside * width, width)]
        return pltpu.make_async_copy(source, landed.at[n], swap_sem.at[n])

    def factor_load(kind, shift):
        source = (all_hidden, all_gate, all_up)[kind].at[shift]
        return pltpu.make_async_copy(source, factors.at[kind // 2, shift - 1], factor_sem.at[kind, shift])

    away = [(n, n // chunks) for n in range(pieces) if place(n)[0] != 0]

    def swap_acts(kind):
        for shift in range(1, groups):
            copy = act_to_group(kind, shift)
            copy.wait_send()
            copy.wait_recv()
            factor_load(kind, shift).start()

    def stage_swap(_):
        for n, kind in away:
            copy = piece_to_group(n, kind, place(n)[0])
            copy.wait_send()
            copy.wait_recv()
            swap_load(n, kind).start()
        swap_acts(0)

    def stage_swap_acts(_):
        swap_acts(1)
        swap_acts(2)

    def summed(kind, i):
        own = (hidden, gate_pre, up_pre)[kind]
        total = None
        for shift in range(groups):
            act = own[...] if shift == 0 else factors[kind // 2, shift - 1]
            piece = landed[(chunks if kind == 0 else 0) + (shift + groups - 1) % groups * per_block + i]
            pair = (act, piece) if kind == 0 else (piece, act)
            term = lax.dot_general(*pair, ROWS_FIRST, preferred_element_type=F32)
            total = term if total is None else total + term
        return total.astype(BF16)

    def sum_out(kind, i):
        at = pl.ds(pl.multiple_of(i * width, 128), width)
        held, target = ((vdown, down_sum.at[:, at]), (vgate, gate_sum.at[at, :]), (vup, up_sum.at[at, :]))[kind]
        return pltpu.make_async_copy(held.at[i], target, sum_sem.at[kind, i])

    def stage_sum_down(i):
        @pl.when(i == 0)
        def _():
            for n, kind in away:
                swap_load(n, kind).wait()
            for shift in range(1, groups):
                factor_load(0, shift).wait()

        vdown[i] = summed(0, i)
        sum_out(0, i).start()

    def stage_sum_gate_up(i):
        @pl.when(i == 0)
        def _():
            for kind in (1, 2):
                for shift in range(1, groups):
                    factor_load(kind, shift).wait()

        vgate[i] = summed(1, i)
        sum_out(1, i).start()
        vup[i] = summed(2, i)
        sum_out(2, i).start()

    _, ahead, relay, multiply, hand, partial, finish_inner, finish_outer = lags
    first_make = chunks + multiply
    stages = [
        (-lead, lead, stage_onward),
        (-ahead, ahead, stage_forward),
        (first_make + partial, 0, stage_partial),
        (first_make, 0, stage_make),
        (0, 0, stage_spread),
        (first_make + hand, 0, stage_hand),
        (relay, 0, stage_relay),
        (multiply, 0, stage_multiply),
        (first_make + finish_inner, 0, stage_finish_inner),
        (first_make + finish_outer, 0, stage_finish_outer),
    ]
    stages = [(lag, first, pieces, stage) for lag, first, stage in stages]
    ticks = first_make + pieces + finish_outer
    if sums:
        begin = first_make + chunks
        stages += [
            (begin + sums[0], 0, 1, stage_swap),
            (begin + sums[1], 0, per_block, stage_sum_down),
            (begin + sums[2], 0, 1, stage_swap_acts),
            (begin + sums[3], 0, per_block, stage_sum_gate_up),
        ]
        ticks = max(ticks, begin + sums[3] + per_block)
    for n in range(ahead):
        stage_forward(n)

    def run_tick(tick, carry):
        for lag, first, end, stage in stages:
            n = tick - lag

            @pl.when((n >= first) & (n < end))
            def _():
                stage(n)

        return carry

    lax.fori_loop(0, ticks, run_tick, 0)

    for n in range(pieces):
        onwards(n, n // chunks).wait_send()
    for n in range(chunks, pieces):
        for copy in planes(n):
            copy.wait_send()
    for m in range(chunks, pieces):
        for copy in mades(m):
            copy.wait_send()
    for m in range(pieces - 4, pieces):
        outs(m, 1).wait()

    @pl.when(inner)
    def _():
        forwards(pieces - 1).wait_send()
        for n in range(chunks, pieces):
            mates(n).wait_send()
        for m in range(chunks, pieces):
            parts(m).wait_send()
            fins(m).wait_send()

    if sums:
        for kind in range(3):
            for i in range(per_block):
                sum_out(kind, i).wait()
        return
    group_copies = [(place(n)[0], piece_to_group(n, n // chunks, place(n)[0])) for n in range(pieces)]
    group_copies += [(shift, act_to_group(kind, shift)) for kind in range(3) for shift in range(groups)]
    for shift, copy in group_copies:
        if shift == 0:
            copy.wait()
        else:
            copy.wait_recv()
            copy.wait_send()


def weights_kernel(
    layer_in, tokens_in, token_cols, grad_cols, all_hidden, all_gate, all_up,
    layer_out, tokens_grad, gate_sum, up_sum, down_sum,
    left, grads, acts, moved, result, load_sem, move_sem, out_sem,
):
    through = ((layer_in, layer_out), (tokens_in, tokens_grad))
    moves = [pltpu.make_async_copy(a, moved.at[i], move_sem.at[i]) for i, (a, _) in enumerate(through)]
    moves_out = [pltpu.make_async_copy(moved.at[i], b, move_sem.at[2 + i]) for i, (_, b) in enumerate(through)]
    pairs = (
        (all_hidden, acts.at[0]), (grad_cols, grads), (token_cols, left), (all_gate, acts.at[1]), (all_up, acts.at[2])
    )
    loads = [pltpu.make_async_copy(a, b, load_sem.at[i]) for i, (a, b) in enumerate(pairs)]
    for copy in loads + moves:
        copy.start()
    depth = left.shape[0] * left.shape[1]
    block = left.shape[2]
    units = acts.shape[3]
    tile = 256
    stores = []

    def matrix(ref, at):
        return ref[:, :, at].reshape(depth, at.size)

    def put(values, target):
        i = len(stores)
        slot = i % 2
        if i >= 2:
            stores[i - 2].wait()
        result[slot, :, 0 : values.shape[1]] = values.astype(BF16)
        copy = pltpu.make_async_copy(result.at[slot, :, pl.ds(0, values.shape[1])], target, out_sem.at[i])
        copy.start()
        stores.append(copy)

    loads[0].wait()
    loads[1].wait()
    for start in range(0, units, tile):
        at = pl.ds(start, tile)
        values = lax.dot_general(
            matrix(acts.at[0], at), matrix(grads, pl.ds(0, block)), ROWS_FIRST, preferred_element_type=F32
        )
        put(values, down_sum.at[at, :])
    for copy, copy_out in zip(moves, moves_out):
        copy.wait()
        copy_out.start()
    loads[2].wait()
    for kind, target in ((1, gate_sum), (2, up_sum)):
        loads[2 + kind].wait()
        for start in range(0, block, tile):
            at = pl.ds(start, tile)
            values = lax.dot_general(
                matrix(left, at), matrix(acts.at[kind], pl.ds(0, units)), ROWS_FIRST, preferred_element_type=F32
            )
            put(values, target.at[at, :])
    for copy in stores[-2:] + moves_out:
        copy.wait()


def move_kernel(*refs):
    sources, targets, held, (in_sem, out_sem) = refs[:5], refs[5:10], refs[10:15], refs[15:]
    ins, outs = [], []
    for part in range(MOVES):
        for i in range(5):
            size = sources[i].shape[0] // MOVES
            at = pl.ds(part * size, size)
            ins.append(pltpu.make_async_copy(sources[i].at[at], held[i].at[at], in_sem.at[i, part]))
            outs.append(pltpu.make_async_copy(held[i].at[at], targets[i].at[at], out_sem.at[i, part]))
    for copy in ins:
        copy.start()
    for copy, copy_out in zip(ins, outs):
        copy.wait()
        copy_out.start()
    for copy in outs:
        copy.wait()


def per_device(tokens, expert_ids, gate_codes, w_gate, w_up, w_down, out_grad):
    experts = lax.axis_size("expert")
    groups = lax.axis_size("dp")
    lanes = experts // LINE
    tok_count, model_width = tokens.shape
    pair_count = tok_count * expert_ids.shape[1]
    capacity = 3 * pair_count // (2 * experts)
    capacity = -(-capacity // 16) * 16
    rows = experts * capacity
    half = lanes * capacity
    chunks = groups * max(1, PIECES // groups)
    ring = chunks // 2
    deep = half <= 96
    slots, lags, sums = (2 * chunks, DEEP, SUMS) if deep else (chunks, SHALLOW, None)
    width = model_width // chunks
    block = model_width // groups
    pieces = 2 * chunks
    gate_matrix, up_matrix, down_matrix = w_gate[0], w_up[0], w_down[0]
    units = gate_matrix.shape[1]
    vmem = pl.BlockSpec(memory_space=pltpu.VMEM)
    anywhere = pl.BlockSpec(memory_space=pl.ANY)
    dma = pltpu.SemaphoreType.DMA

    def shape(*dims):
        return jax.ShapeDtypeStruct(dims, BF16)

    def buffer(*dims):
        return pltpu.VMEM(dims, BF16)

    peers = max(1, lanes - 1)
    layer_out, tokens_grad, *others = pl.pallas_call(
        functools.partial(exchange_kernel, lanes, capacity, groups, chunks, ring, slots, lags, sums),
        out_shape=(
            shape(tok_count, model_width),
            shape(tok_count, model_width),
            shape(groups, rows, block),
            shape(groups, rows, block),
            shape(groups, rows, units),
            shape(groups, rows, units),
            shape(groups, rows, units),
            shape(block, units),
            shape(block, units),
            shape(units, block),
        ),
        in_specs=[vmem] * 2 + [anywhere] * 5,
        out_specs=(anywhere,) * 10,
        scratch_shapes=[
            pltpu.VMEM((LINE, 2 * experts, tok_count), F32),
            buffer(LINE, chunks, tok_count, width),
            buffer(2, LINE, 2 * half, tok_count),
            buffer(2, LINE, tok_count, 2 * half),
            buffer(2, tok_count, half),
            buffer(chunks, lanes, LINE * capacity, width),
            buffer(chunks, lanes, 3 * capacity, width),
            buffer(pieces, rows, width),
            pltpu.VMEM((rows, units), F32),
            pltpu.VMEM((rows, units), F32),
            pltpu.VMEM((rows, units), F32),
            buffer(rows, units),
            buffer(rows, units),
            buffer(rows, units),
            buffer(chunks, units, width),
            buffer(ring, width, units),
            buffer(ring, width, units),
            buffer(chunks, lanes, LINE, capacity, width),
            buffer(slots, LINE, 2 * half, width),
            buffer(chunks, 2, tok_count, width),
            buffer(slots, 2, tok_count, width),
            buffer(chunks, tok_count, width),
            buffer(4, tok_count, width),
            buffer(2, groups - 1, rows, units) if sums else buffer(16, 128),
            dma((2,)),
            dma((LINE,)),
            dma((pieces,)),
            dma((pieces,)),
            dma((pieces, LINE)),
            dma((pieces,)),
            dma((pieces, peers)),
            dma((pieces, peers)),
            dma((pieces,)),
            dma((pieces,)),
            dma((pieces, peers)),
            dma((pieces, peers)),
            dma((pieces, 2)),
            dma((pieces, 2)),
            dma((pieces,)),
            dma((pieces,)),
            dma((pieces,)),
            dma((pieces,)),
            dma((pieces,)),
            dma((pieces, 2)),
            dma((chunks,)),
            dma((pieces,)),
            dma((pieces,)),
            dma((3, groups)),
            dma((3, groups)),
            dma((pieces,)),
            dma((3, groups)),
            dma((3, chunks // groups)),
        ],
        compiler_params=pltpu.CompilerParams(
            collective_id=0, has_side_effects=True, vmem_limit_bytes=63 * MIB
        ),
    )(expert_ids.T, gate_codes.T, tokens, out_grad, gate_matrix, up_matrix, down_matrix)

    if sums:
        results = [layer_out, tokens_grad, *others[5:]]
        layer_out, tokens_grad, gate_sum, up_sum, down_sum = pl.pallas_call(
            move_kernel,
            out_shape=tuple(shape(*result.shape) for result in results),
            in_specs=[anywhere] * 5,
            out_specs=(anywhere,) * 5,
            scratch_shapes=[buffer(*result.shape) for result in results] + [dma((5, MOVES)), dma((5, MOVES))],
            compiler_params=pltpu.CompilerParams(vmem_limit_bytes=60 * MIB),
        )(*results)
        return layer_out, tokens_grad, gate_sum[None], up_sum[None], down_sum[None]

    outs = pl.pallas_call(
        weights_kernel,
        out_shape=(
            shape(tok_count, model_width),
            shape(tok_count, model_width),
            shape(block, units),
            shape(block, units),
            shape(units, block),
        ),
        in_specs=[anywhere] * 7,
        out_specs=(anywhere,) * 5,
        scratch_shapes=[
            buffer(groups, rows, block),
            buffer(groups, rows, block),
            buffer(3, groups, rows, units),
            buffer(2, tok_count, model_width),
            buffer(2, 256, max(block, units)),
            dma((5,)),
            dma((4,)),
            dma((units // 256 + 2 * (block // 256),)),
        ],
        compiler_params=pltpu.CompilerParams(vmem_limit_bytes=56 * MIB),
    )(layer_out, tokens_grad, *others[:5])
    layer_out, tokens_grad, gate_sum, up_sum, down_sum = outs
    return layer_out, tokens_grad, gate_sum[None], up_sum[None], down_sum[None]


def solution(mesh):
    placed = (
        P(("dp", "expert"), None),
        P(("dp", "expert"), None),
        P(("dp", "expert"), None),
        P("expert", None, None),
        P("expert", None, None),
        P("expert", None, None),
        P(("dp", "expert"), None),
    )
    return jax.shard_map(
        per_device,
        mesh=mesh,
        in_specs=placed,
        out_specs=(
            P(("dp", "expert"), None),
            P(("dp", "expert"), None),
            P("expert", "dp", None),
            P("expert", "dp", None),
            P("expert", None, "dp"),
        ),
        check_vma=False,
    )
```
